32 devices in a mesh: grp: 2 (over y), cls: 8 (over z, x), ori: 2 (over core).
Axes of the slice: x: 2, y: 2, z: 4, core: 2. Of those that a mesh axis runs over, the one named last changes fastest.
Arguments:
- particles: bfloat16 [512, 16384], P(('grp', 'cls')), parts along dimension 0, may hold values from -6 to 6
- tau: bfloat16 [512], P(('grp', 'cls')), parts along dimension 0, may hold values from 0.019897461 to 0.079589844
- candidates: int32 [512, 2], P(('grp', 'cls')), parts along dimension 0, may hold values from 0 to 7, all different within a row; in each aligned block of 32 rows (0 to 31, 32 to 63, ...) at most 16 rows name the same one
- prune: int32 [512, 256], P(('grp', 'cls'), 'ori'), parts along dimension 0, may hold values from 0 to 1, as said below
- projections: bfloat16 [8, 256, 16384], P('cls', 'ori'), may hold values from -6 to 6
Outputs:
- expected: bfloat16 [512, 16384], P(('grp', 'cls'), 'ori'), parts along dimension 0
The draws below stay inside these ranges and needn't reach their ends.
There are 2 independent parts, one for each index of `grp`. The reference program is written for one: setup_inputs(seed, part) draws one part's arguments, and reference() takes and returns one part's arrays. A program takes and returns all parts, laid end to end along the dimension named above; an argument that names none is the same for every part. Nothing has to cross between parts.
Inputs may be any that keep to these rules, and one draw needn't show every extreme that they name: `candidates`: within the rows of one device no class is named by more than 16 rows, a bound that some block reaches; the 2 classes of a row differ. `prune`: every particle keeps at least one orientation.
All inputs are finite; a program needn't handle non-finite values.
Results may differ from the reference program's by a relative error of at most 0.0034.
Values may be sent and summed in bfloat16 or wider, within the bound.
No kernel may reach another device: no remote copies, remote signals or barrier semaphores. Data moves between devices by JAX's collectives and lax.ppermute only.
A program may use at most 128 MiB of HBM per device.

```python
import math
import jax
import jax.numpy as jnp
import numpy as np
from jax import lax

BOX = 128
PIX = 16384
PART_DEV = 32
TOP = 2
CLASSES = 8
ORIENTS = 256
PARTICLES = 256
CAP = 16


def draw_prune(key, part):
    first_key, second_key = jax.random.split(key)
    coin_flips = jax.random.randint(first_key, (PARTICLES, ORIENTS), 0, 2)
    picked = jax.random.randint(second_key, (PARTICLES, 1), 0, ORIENTS)
    forced = (jnp.arange(ORIENTS, dtype=jnp.int32)[None, :] == picked).astype(jnp.int32)
    return jnp.maximum(coin_flips, forced).astype(jnp.int32)


def unit_entries(entry_key, shape):
    values = jax.random.truncated_normal(entry_key, -6.0, 6.0, shape, jnp.float32)
    return values


def draw_particles(key, part):
    image_key = jax.random.fold_in(key, 11)
    return unit_entries(image_key, (PARTICLES, PIX)).astype(jnp.bfloat16)


def draw_projections(key, part):
    base_key = jax.random.fold_in(key, 23)

    def one_class(class_index):
        class_key = jax.random.fold_in(base_key, class_index)
        return unit_entries(class_key, (ORIENTS, PIX)).astype(jnp.bfloat16)
    return lax.map(one_class, jnp.arange(CLASSES, dtype=jnp.int32))


def levels(own_key, dims, shards, smallest, high):
    factor_of = 1.0
    for dim, blocks in shards:
        heights = jax.random.uniform(jax.random.fold_in(jax.random.fold_in(own_key, 6), dim), (blocks,), jnp.float32, smallest / len(shards), high / len(shards))
        factor_of = factor_of * jnp.repeat(jnp.exp(heights), dims[dim] // blocks).reshape((-1,) + (1,) * (len(dims) - 1 - dim))
    return factor_of


def deal_out(own_key, own, number, rows, amount, top, most, lean):
    sequence = jax.random.permutation(own_key, amount)
    crowded, common = load_shares(amount, rows * top, most, lean, True), load_shares(amount, rows * top, most, lean, False)
    places = jnp.arange(amount)

    def named(lengths, turn):
        used = int((lengths > 0).sum())
        fixed = max(1, used // 4)
        passed = fixed + (places - fixed + turn * (used - fixed)) % max(1, amount - fixed)
        return jnp.zeros((amount,), jnp.int32).at[sequence[jnp.where(places < fixed, places, passed)]].set(jnp.asarray(lengths, jnp.int32))

    lengths = jnp.where(number % 4 == 0, named(crowded, number // 4), named(common, number - number // 4 - 1))
    mixed = jax.random.permutation(jax.random.fold_in(own, 3), amount)
    giver, taker = mixed[0:amount // 2 * 2:2], mixed[1:amount // 2 * 2:2]
    room = jnp.minimum(lengths[giver] - 1, most - lengths[taker]) // 2
    room = jnp.where((giver == sequence[0]) | (taker == sequence[0]) | (lengths[taker] == 0), 0, jnp.maximum(room, 0))
    passed = jax.random.randint(jax.random.fold_in(own, 4), (amount // 2,), 0, 1 << 20) % (room + 1)
    lengths = lengths.at[giver].add(-passed).at[taker].add(passed)
    members = jnp.searchsorted(jnp.cumsum(lengths), jnp.arange(rows * top), side="right").astype(jnp.int32)
    grid = members.reshape(top, rows).T
    grid = grid[jax.random.permutation(jax.random.fold_in(own, 1), rows)]
    turn = jax.random.randint(jax.random.fold_in(own, 2), (rows, 1), 0, top)
    return jnp.take_along_axis(grid, (jnp.arange(top)[None, :] + turn) % top, axis=1)


def load_shares(count, total, bound, slope, full):
    portions = [(1 << 20) // math.isqrt(rank ** slope) + 1 for rank in range(1, count + 1)]
    largest = bound if full else min(bound, max(-(-total // count), total * portions[0] // sum(portions)))
    least = 1 if total - largest >= count - 1 else 0
    counts, surplus = [largest] + [least] * (count - 1), total - largest - least * (count - 1)
    while surplus > 0:
        free = [i for i in range(1, count) if counts[i] < largest] or [i for i in range(1, count) if counts[i] < bound]
        pool, remaining = sum([portions[i] for i in free]), surplus
        for i in free:
            addition = min(bound - counts[i], max(1, remaining * portions[i] // pool), surplus)
            counts[i] = counts[i] + addition
            surplus = surplus - addition
    return np.array(counts)


def setup_inputs(seed: int = 0, part: int = 0) -> dict:
    splits = jax.random.split(jax.random.key(seed), 6)
    part_keys = jax.random.split(jax.random.fold_in(splits[5], part), 6)
    particles = draw_particles(jax.random.fold_in(jax.random.fold_in(splits[5], part), 71), part)
    tau = jnp.clip(jnp.exp(math.log(0.079589844) - 1.3862944 * jax.random.uniform(part_keys[1], (PARTICLES,), jnp.float32) ** levels(part_keys[1], (PARTICLES,), ((0, 8),), -0.2, 0.2)), 0.019897461, 0.079589844).astype(jnp.bfloat16)
    candidates_keys = jax.random.split(jax.random.fold_in(part_keys[2], 1), PARTICLES // PART_DEV)
    candidates_turns = jax.random.permutation(jax.random.fold_in(part_keys[2], 3), PARTICLES // PART_DEV)
    candidates = jax.vmap(lambda own, number: deal_out(jax.random.fold_in(part_keys[2], 2), own, number, PART_DEV, CLASSES, TOP, CAP, 2))(candidates_keys, candidates_turns).reshape((PARTICLES, TOP))
    prune = draw_prune(jax.random.fold_in(jax.random.fold_in(splits[5], part), 71), part)
    projections = draw_projections(jax.random.fold_in(splits[5], 71), part)
    return {"particles": particles, "tau": tau, "candidates": candidates, "prune": prune, "projections": projections}


shift_table = ((0, 0), (1, 0), (-1, 0), (0, 1), (0, -1))


def reference(particles, tau, candidates, prune, projections):
    shift_count = len(shift_table)

    def one_block(pieces):
        images, scales, chosen, keep_rows = pieces
        width = images.shape[0]
        grid_rows = images.astype(jnp.float32).reshape(width, BOX, BOX)
        rolled = jnp.stack([jnp.roll(grid_rows, (-offset[0], -offset[1]), axis=(1, 2)) for offset in shift_table], axis=1)
        rolled = rolled.reshape(width, shift_count, PIX)
        chosen_proj = projections[chosen].astype(jnp.float32)
        row_norms = jnp.sum(chosen_proj * chosen_proj, axis=-1)
        products = jnp.einsum('bsp,bcop->bcso', rolled, chosen_proj)
        scores = scales.astype(jnp.float32)[:, None, None, None] * (products - 0.5 * row_norms[:, :, None, :])
        keep_all = (keep_rows > 0)[:, None, None, :]
        peak_score = jnp.max(jnp.where(keep_all, scores, jnp.float32(-1e30)), axis=(2, 3))
        weights = jnp.exp(jnp.where(keep_all, scores - peak_score[:, :, None, None], -jnp.inf)).astype(jnp.bfloat16)
        weight_total = jnp.sum(weights.astype(jnp.float32), axis=(2, 3))
        summed = jnp.einsum('bcso,bcop->bcsp', weights.astype(jnp.float32), chosen_proj)
        summed = summed.reshape(width, TOP, shift_count, BOX, BOX)
        field = jnp.zeros((width, TOP, BOX, BOX), summed.dtype)
        for index, offset in enumerate(shift_table):
            field = field + jnp.roll(summed[:, :, index], offset, axis=(2, 3))
        unit_image = field.reshape(width, TOP, PIX) / weight_total[:, :, None]
        log_weight = peak_score + jnp.log(weight_total)
        best_log = jnp.max(log_weight, axis=1, keepdims=True)
        factors = jnp.exp(log_weight - best_log)
        result = jnp.sum(factors[:, :, None] * unit_image, axis=1) / jnp.sum(factors, axis=1)[:, None]
        return result.astype(jnp.bfloat16)

    block_rows = 4
    block_count = PARTICLES // block_rows
    stacked = lax.map(one_block, (particles.reshape(block_count, block_rows, PIX),
                                  tau.reshape(block_count, block_rows),
                                  candidates.reshape(block_count, block_rows, TOP),
                                  prune.reshape(block_count, block_rows, ORIENTS)))
    return stacked.reshape(PARTICLES, PIX)
```

```python
import functools

import jax
import jax.numpy as jnp
from jax import lax
from jax.experimental import pallas as pl
from jax.experimental.pallas import tpu as pltpu
from jax.sharding import Mesh
from jax.sharding import PartitionSpec as P

BOX = 128
LANES = 128
NEG = -1e30
shift_count = 5
VMEM_LIMIT = 48 * 1024 * 1024


def split3(value):
    high = value.astype(jnp.bfloat16)
    rest = value - high.astype(jnp.float32)
    middle = rest.astype(jnp.bfloat16)
    low = (rest - middle.astype(jnp.float32)).astype(jnp.bfloat16)
    return high, middle, low


def put_log(value, rows):
    high, middle, low = split3(value)
    lane = lax.broadcasted_iota(jnp.int32, (rows, LANES), 1)
    pieces = jnp.where(
        lane == 0,
        high.astype(jnp.float32),
        jnp.where(
            lane == 1,
            middle.astype(jnp.float32),
            jnp.where(lane == 2, low.astype(jnp.float32), 0.0),
        ),
    )
    return pieces.astype(jnp.bfloat16)


def get_log(pieces):
    wide = pieces.astype(jnp.float32)
    return (wide[:, 0:1] + wide[:, 1:2]) + wide[:, 2:3]


def column_to_row(column, count):
    eye = lax.broadcasted_iota(jnp.int32, (count, count), 0) == lax.broadcasted_iota(
        jnp.int32, (count, count), 1
    )
    return jnp.sum(jnp.where(eye, column, 0.0), axis=0, keepdims=True)


def roll_lanes(block, amount):
    pieces = [
        pltpu.roll(block[:, start : start + LANES], amount % LANES, 1)
        for start in range(0, block.shape[1], LANES)
    ]
    return jnp.concatenate(pieces, axis=1)


def pack_kernel(base_ref, meta_ref, x_ref, out_ref, choice_ref, choice_scr, *, classes, cap, choose):
    @pl.when(pl.program_id(0) == 0)
    def _():
        rows = meta_ref.shape[0]
        slots = classes * cap
        meta = meta_ref[...].astype(jnp.float32)
        base = base_ref[0]
        ids = (lax.broadcasted_iota(jnp.int32, (rows, classes), 1) + base).astype(jnp.float32)
        named = jnp.zeros((rows, classes), jnp.float32)
        for j in range(choose):
            named = jnp.where(meta[:, 1 + j : 2 + j] == ids, 1.0, named)
        earlier = (
            lax.broadcasted_iota(jnp.int32, (rows, rows), 0)
            > lax.broadcasted_iota(jnp.int32, (rows, rows), 1)
        ).astype(jnp.float32)
        rank = jnp.dot(earlier, named, preferred_element_type=jnp.float32)
        slot = lax.broadcasted_iota(jnp.int32, (classes, slots), 1)
        first = lax.broadcasted_iota(jnp.int32, (classes, slots), 0) * cap
        spread = ((slot >= first) & (slot < first + cap)).astype(jnp.float32)
        rank_at = jnp.dot(rank, spread, preferred_element_type=jnp.float32)
        named_at = jnp.dot(named, spread, preferred_element_type=jnp.float32)
        place = (lax.broadcasted_iota(jnp.int32, (rows, slots), 1) % cap).astype(jnp.float32)
        choice = jnp.where((named_at > 0.5) & (rank_at == place), 1.0, 0.0)
        choice_scr[...] = choice
        choice_ref[...] = choice

    out_ref[...] = lax.dot_general(
        choice_scr[...].astype(jnp.bfloat16),
        x_ref[...],
        (((0,), (0,)), ((), ())),
        preferred_element_type=jnp.float32,
    ).astype(jnp.bfloat16)


def pack(base, payload, classes, cap, choose):
    rows, width = payload.shape
    slots = classes * cap
    tile = 1408
    return pl.pallas_call(
        functools.partial(pack_kernel, classes=classes, cap=cap, choose=choose),
        grid_spec=pltpu.PrefetchScalarGridSpec(
            num_scalar_prefetch=1,
            grid=(width // tile,),
            in_specs=[
                pl.BlockSpec((rows, LANES), lambda i, b: (0, width // LANES - 1)),
                pl.BlockSpec((rows, tile), lambda i, b: (0, i)),
            ],
            out_specs=[
                pl.BlockSpec((slots, tile), lambda i, b: (0, i)),
                pl.BlockSpec((rows, slots), lambda i, b: (0, 0)),
            ],
            scratch_shapes=[pltpu.VMEM((rows, slots), jnp.float32)],
        ),
        out_shape=[
            jax.ShapeDtypeStruct((slots, width), jnp.bfloat16),
            jax.ShapeDtypeStruct((rows, slots), jnp.float32),
        ],
        compiler_params=pltpu.CompilerParams(vmem_limit_bytes=VMEM_LIMIT),
        name="pack",
    )(base, payload, payload)


def norm_kernel(own_ref, other_ref, out_ref, acc):
    step = pl.program_id(0)

    @pl.when(step == 0)
    def _():
        acc[...] = jnp.zeros_like(acc)

    both = jnp.concatenate([own_ref[...], other_ref[...]], axis=0).astype(jnp.float32)
    square = both * both
    total = square[:, 0:LANES]
    for start in range(LANES, square.shape[1], LANES):
        total = total + square[:, start : start + LANES]
    acc[...] += total

    @pl.when(step == pl.num_programs(0) - 1)
    def _():
        out_ref[...] = column_to_row(jnp.sum(acc[...], axis=1, keepdims=True), acc.shape[0])


def half_norms(own, other, pixels):
    count = own.shape[0]
    tile = 1024
    window = pl.BlockSpec((pl.Element(count), pl.Element(tile)), lambda k: (0, (k * (tile // LANES) + 1) * LANES))
    return pl.pallas_call(
        norm_kernel,
        grid=(pixels // tile,),
        in_specs=[window, window],
        out_specs=pl.BlockSpec((1, 2 * count), lambda k: (0, 0)),
        out_shape=jax.ShapeDtypeStruct((1, 2 * count), jnp.float32),
        scratch_shapes=[pltpu.VMEM((2 * count, LANES), jnp.float32)],
        compiler_params=pltpu.CompilerParams(vmem_limit_bytes=VMEM_LIMIT),
        name="half_norms",
    )(own, other)


def score_kernel(x_ref, keep_ref, own_ref, other_ref, norm_ref, out_ref):
    step = pl.program_id(0)
    rows, tile = x_ref.shape
    count = own_ref.shape[0]

    @pl.when(step == 0)
    def _():
        out_ref[...] = jnp.zeros_like(out_ref)

    image = x_ref[...]
    wide = image.astype(jnp.float32)
    left = roll_lanes(wide, -1).astype(jnp.bfloat16)
    right = roll_lanes(wide, 1).astype(jnp.bfloat16)
    both = jnp.concatenate([own_ref[...], other_ref[...]], axis=0)
    dims = (((1,), (1,)), ((), ()))

    def product(lhs, start):
        return lax.dot_general(
            lhs, both[:, start : start + tile], dims, preferred_element_type=jnp.float32
        )

    stacked = product(jnp.concatenate([image, left, right], axis=0), LANES)
    span = 2 * count
    out_ref[:, 0:span] += stacked[0:rows]
    out_ref[:, span : 2 * span] += product(image, 0)
    out_ref[:, 2 * span : 3 * span] += product(image, 2 * LANES)
    out_ref[:, 3 * span : 4 * span] += stacked[rows : 2 * rows]
    out_ref[:, 4 * span : 5 * span] += stacked[2 * rows : 3 * rows]

    @pl.when(step == pl.num_programs(0) - 1)
    def _():
        barred = jnp.where(keep_ref[...].astype(jnp.float32) > 0.5, 0.0, NEG)
        offset = jnp.concatenate([barred, jnp.zeros_like(barred)], axis=1) - 0.5 * norm_ref[...]
        for index in range(shift_count):
            out_ref[:, index * span : (index + 1) * span] += offset


def half_scores(records, own, other, norms, pixels):
    rows, width = records.shape
    count = own.shape[0]
    tile = 1024
    window = pl.BlockSpec((pl.Element(count), pl.Element(tile + 2 * LANES)), lambda k: (0, k * tile))
    return pl.pallas_call(
        score_kernel,
        grid=(pixels // tile,),
        in_specs=[
            pl.BlockSpec((rows, tile), lambda k: (0, k)),
            pl.BlockSpec((rows, count), lambda k: (0, pixels // count)),
            window,
            window,
            pl.BlockSpec((1, 2 * count), lambda k: (0, 0)),
        ],
        out_specs=pl.BlockSpec((rows, 2 * shift_count * count), lambda k: (0, 0)),
        out_shape=jax.ShapeDtypeStruct((rows, 2 * shift_count * count), jnp.float32),
        compiler_params=pltpu.CompilerParams(vmem_limit_bytes=VMEM_LIMIT),
        name="half_scores",
    )(records, records, own, other, norms)


def mean_kernel(mine_ref, theirs_ref, meta_ref, own_ref, other_ref, out_ref, weight_scr, inv_scr, log_scr):
    step = pl.program_id(0)
    rows, tile = out_ref.shape
    count = own_ref.shape[0]
    span = 2 * count

    @pl.when(step == 0)
    def _():
        tau = meta_ref[:, 0:1].astype(jnp.float32)
        scores = []
        peak = jnp.full((rows, 1), NEG, jnp.float32)
        for index in range(shift_count):
            mine = mine_ref[:, index * span : (index + 1) * span]
            theirs = theirs_ref[:, index * span : (index + 1) * span]
            swapped = jnp.concatenate([theirs[:, count:], theirs[:, :count]], axis=1)
            full = mine + swapped
            score = jnp.where(full > -1e29, tau * full, NEG)
            scores.append(score)
            peak = jnp.maximum(peak, jnp.max(score, axis=1, keepdims=True))
        total = jnp.zeros((rows, 1), jnp.float32)
        for index, place in enumerate((0, 3, 4, 1, 2)):
            score = scores[index]
            weight = jnp.where(score > -1e28, jnp.exp(score - peak), 0.0).astype(jnp.bfloat16)
            total = total + jnp.sum(weight.astype(jnp.float32), axis=1, keepdims=True)
            weight_scr[place * rows : (place + 1) * rows, :] = weight
        filled = total > 0
        safe = jnp.where(filled, total, 1.0)
        inv_scr[...] = jnp.broadcast_to(1.0 / safe, inv_scr.shape)
        log_scr[...] = put_log(jnp.where(filled, peak + jnp.log(safe), NEG), rows)

    both = jnp.concatenate([own_ref[...], other_ref[...]], axis=0)

    def product(lhs, start):
        return jnp.dot(lhs, both[:, start : start + tile], preferred_element_type=jnp.float32)

    stacked = product(weight_scr[0 : 3 * rows, :], LANES)
    mean = stacked[0:rows]
    mean = mean + product(weight_scr[3 * rows : 4 * rows, :], 0)
    mean = mean + product(weight_scr[4 * rows : 5 * rows, :], 2 * LANES)
    mean = mean + roll_lanes(stacked[rows : 2 * rows], 1)
    mean = mean + roll_lanes(stacked[2 * rows : 3 * rows], -1)
    out_ref[...] = (mean * inv_scr[:, 0:1]).astype(jnp.bfloat16)

    @pl.when(step == pl.num_programs(0) - 1)
    def _():
        out_ref[:, tile - LANES :] = log_scr[...]


def weighted_means(mine, theirs, records, own, other, pixels):
    rows, width = records.shape
    count = own.shape[0]
    out_width = pixels + LANES
    tile = 13 * LANES
    window = pl.BlockSpec((pl.Element(count), pl.Element(tile + 2 * LANES)), lambda k: (0, k * tile))
    whole = pl.BlockSpec(mine.shape, lambda k: (0, 0))
    return pl.pallas_call(
        mean_kernel,
        grid=(out_width // tile,),
        in_specs=[
            whole,
            whole,
            pl.BlockSpec((rows, LANES), lambda k: (0, width // LANES - 1)),
            window,
            window,
        ],
        out_specs=pl.BlockSpec((rows, tile), lambda k: (0, k)),
        out_shape=jax.ShapeDtypeStruct((rows, out_width), jnp.bfloat16),
        scratch_shapes=[
            pltpu.VMEM((shift_count * rows, 2 * count), jnp.bfloat16),
            pltpu.VMEM((rows, LANES), jnp.float32),
            pltpu.VMEM((rows, LANES), jnp.bfloat16),
        ],
        compiler_params=pltpu.CompilerParams(vmem_limit_bytes=VMEM_LIMIT),
        name="weighted_means",
    )(mine, theirs, records, own, other)


def mix_kernel(*refs, dense, logs):
    if dense:
        choice_ref, back_log_ref, back_ref, part_log_ref, part_ref, out_ref, mix_scr, log_scr = refs
    else:
        choice_ref, back_log_ref, back_ref, out_ref, mix_scr, log_scr = refs
    step = pl.program_id(0)
    rows, slots = choice_ref.shape

    @pl.when(step == 0)
    def _():
        chosen = choice_ref[...] > 0.5
        row = column_to_row(get_log(back_log_ref[...]), slots)
        value = jnp.where(chosen, row, NEG)
        best = jnp.max(value, axis=1, keepdims=True)
        if dense:
            part = get_log(part_log_ref[...])
            best = jnp.maximum(best, part)
        factor = jnp.where(chosen, jnp.exp(value - best), 0.0)
        total = jnp.sum(factor, axis=1, keepdims=True)
        if dense:
            part_factor = jnp.where(part > -1e29, jnp.exp(part - best), 0.0)
            total = total + part_factor
            eye = lax.broadcasted_iota(jnp.int32, (rows, rows), 0) == lax.broadcasted_iota(
                jnp.int32, (rows, rows), 1
            )
            factor = jnp.concatenate([factor, jnp.where(eye, part_factor, 0.0)], axis=1)
        filled = total > 0
        safe = jnp.where(filled, total, 1.0)
        high, middle, low = split3(factor / safe)
        mix_scr[0:rows, :] = high
        mix_scr[rows : 2 * rows, :] = middle
        mix_scr[2 * rows : 3 * rows, :] = low
        log_scr[...] = put_log(jnp.where(filled, best + jnp.log(safe), NEG), rows)

    images = back_ref[...]
    if dense:
        images = jnp.concatenate([images, part_ref[...]], axis=0)
    mixed = jnp.dot(mix_scr[...], images, preferred_element_type=jnp.float32)
    mixed = mixed[0:rows] + (mixed[rows : 2 * rows] + mixed[2 * rows : 3 * rows])
    out_ref[...] = mixed.astype(jnp.bfloat16)
    if logs:

        @pl.when(step == pl.num_programs(0) - 1)
        def _():
            out_ref[:, out_ref.shape[1] - LANES :] = log_scr[...]


def mix(choice, back, part, pixels):
    rows, slots = choice.shape
    width = back.shape[1]
    dense = part is not None
    logs = not dense
    out_width = pixels + LANES if logs else pixels
    tile = 13 * LANES if logs else 16 * LANES
    last = width // LANES - 1
    in_specs = [
        pl.BlockSpec((rows, slots), lambda k: (0, 0)),
        pl.BlockSpec((slots, LANES), lambda k: (0, last)),
        pl.BlockSpec((slots, tile), lambda k: (0, k)),
    ]
    args = [choice, back, back]
    if dense:
        in_specs += [
            pl.BlockSpec((rows, LANES), lambda k: (0, last)),
            pl.BlockSpec((rows, tile), lambda k: (0, k)),
        ]
        args += [part, part]
    terms = slots + (rows if dense else 0)
    return pl.pallas_call(
        functools.partial(mix_kernel, dense=dense, logs=logs),
        grid=(out_width // tile,),
        in_specs=in_specs,
        out_specs=pl.BlockSpec((rows, tile), lambda k: (0, k)),
        out_shape=jax.ShapeDtypeStruct((rows, out_width), jnp.bfloat16),
        scratch_shapes=[
            pltpu.VMEM((3 * rows, terms), jnp.bfloat16),
            pltpu.VMEM((rows, LANES), jnp.bfloat16),
        ],
        compiler_params=pltpu.CompilerParams(vmem_limit_bytes=VMEM_LIMIT),
        name="mix_final" if dense else "mix_half",
    )(*args)


def trade(block, peers):
    cap = block.shape[0] // peers
    if peers > 4:
        parts = block.reshape(peers, cap, block.shape[1])
        parts = lax.all_to_all(parts, "lo", split_axis=0, concat_axis=0, tiled=True)
        return parts.reshape(block.shape)
    own = lax.axis_index("lo")
    got = [lax.dynamic_slice_in_dim(block, own * cap, cap, axis=0)]
    for flip in range(1, peers):
        piece = lax.dynamic_slice_in_dim(block, (own ^ flip) * cap, cap, axis=0)
        got.append(lax.ppermute(piece, "lo", [(i, i ^ flip) for i in range(peers)]))
    return jnp.concatenate(got, axis=0)


def restore(block, peers):
    cap = block.shape[0] // peers
    if peers > 4:
        parts = block.reshape(peers, cap, block.shape[1])
        parts = lax.all_to_all(parts, "lo", split_axis=0, concat_axis=0, tiled=True)
        return parts.reshape(block.shape)
    own = lax.axis_index("lo")
    got = [block[:cap]]
    for flip in range(1, peers):
        piece = block[flip * cap : (flip + 1) * cap]
        got.append(lax.ppermute(piece, "lo", [(i, i ^ flip) for i in range(peers)]))
    out = jnp.zeros_like(block)
    for flip in range(peers):
        out = lax.dynamic_update_slice_in_dim(out, got[flip], (own ^ flip) * cap, axis=0)
    return out


def on_device(particles, tau, candidates, prune, projections):
    halves = lax.axis_size("hi")
    peers = lax.axis_size("lo")
    cores = lax.axis_size("ori")
    core = lax.axis_index("ori")
    part_rows, choose = candidates.shape
    pixels = particles.shape[1] // cores
    count = prune.shape[1]
    cap = 2 * part_rows * choose // (halves * peers)
    base = (lax.axis_index("hi") * peers).astype(jnp.int32).reshape(1)
    across = [(i, (i + 1) % halves) for i in range(halves)]
    swap = [(i, (i + 1) % cores) for i in range(cores)]

    image_part = lax.dynamic_slice_in_dim(particles, core * pixels, pixels, axis=1)
    meta = jnp.concatenate([tau[:, None], candidates.astype(jnp.bfloat16)], axis=1)
    meta = jnp.pad(meta, ((0, 0), (0, LANES - meta.shape[1])))
    payload = jnp.concatenate([image_part, prune.astype(jnp.bfloat16), meta], axis=1)
    far_payload = lax.ppermute(payload, "hi", across)

    sent_near, choice_near = pack(base, payload, peers, cap, choose)
    records_near = trade(sent_near, peers)

    views = projections[0]
    wide = jnp.concatenate([views[:, -BOX:], views, views[:, : 2 * BOX]], axis=1)
    length = pixels + 3 * BOX
    own_views = lax.dynamic_slice_in_dim(wide, core * pixels, length, axis=1)
    lent_views = lax.dynamic_slice_in_dim(wide, (1 - core) * pixels, length, axis=1)
    other_views = lax.ppermute(lent_views, "ori", swap)
    norms = half_norms(own_views, other_views, pixels)

    def answer(records):
        mine = half_scores(records, own_views, other_views, norms, pixels)
        theirs = lax.ppermute(mine, "ori", swap)
        return weighted_means(mine, theirs, records, own_views, other_views, pixels)

    back_near = restore(answer(records_near), peers)

    sent_far, choice_far = pack(base, far_payload, peers, cap, choose)
    records_far = trade(sent_far, peers)
    back_far = restore(answer(records_far), peers)
    far_mix = mix(choice_far, back_far, None, pixels)
    part_mix = lax.ppermute(far_mix, "hi", across)
    return mix(choice_near, back_near, part_mix, pixels)


def solution(mesh):
    grp, cls, ori = (mesh.shape[name] for name in ("grp", "cls", "ori"))
    inner = Mesh(mesh.devices.reshape(grp, 2, cls // 2, ori), ("grp", "hi", "lo", "ori"))
    rows = ("grp", "hi", "lo")
    placed = (
        P(rows, None),
        P(rows),
        P(rows, None),
        P(rows, "ori"),
        P(("hi", "lo"), "ori", None),
    )
    return jax.shard_map(
        on_device, mesh=inner, in_specs=placed, out_specs=P(rows, "ori"), check_vma=False
    )
```

```python
import functools

import jax
import jax.numpy as jnp
from jax import lax
from jax.experimental import pallas as pl
from jax.experimental.pallas import tpu as pltpu
from jax.sharding import Mesh
from jax.sharding import PartitionSpec as P

BOX = 128
LANES = 128
NEG = -1e30
shift_count = 5
VMEM_LIMIT = 24 * 1024 * 1024
IN_HBM = pl.BlockSpec(memory_space=pltpu.HBM)
IN_VMEM = pl.BlockSpec(memory_space=pltpu.VMEM)


def in_hbm(array):
    return pltpu.with_memory_space_constraint(array, pltpu.HBM)


def joined(refs, start, stop):
    if len(refs) == 1:
        return refs[0][:, start:stop]
    return jnp.concatenate([ref[:, start:stop] for ref in refs], axis=0)


def piece_count(peers):
    return peers if peers <= 4 else 1


def split3(value):
    high = value.astype(jnp.bfloat16)
    rest = value - high.astype(jnp.float32)
    middle = rest.astype(jnp.bfloat16)
    low = (rest - middle.astype(jnp.float32)).astype(jnp.bfloat16)
    return high, middle, low


def put_log(value, rows):
    high, middle, low = split3(value)
    lane = lax.broadcasted_iota(jnp.int32, (rows, LANES), 1)
    pieces = jnp.where(
        lane == 0,
        high.astype(jnp.float32),
        jnp.where(
            lane == 1,
            middle.astype(jnp.float32),
            jnp.where(lane == 2, low.astype(jnp.float32), 0.0),
        ),
    )
    return pieces.astype(jnp.bfloat16)


def get_log(pieces):
    wide = pieces.astype(jnp.float32)
    return (wide[:, 0:1] + wide[:, 1:2]) + wide[:, 2:3]


def column_to_row(column, count):
    eye = lax.broadcasted_iota(jnp.int32, (count, count), 0) == lax.broadcasted_iota(
        jnp.int32, (count, count), 1
    )
    return jnp.sum(jnp.where(eye, column, 0.0), axis=0, keepdims=True)


def roll_lanes(block, amount):
    pieces = [
        pltpu.roll(block[:, start : start + LANES], amount % LANES, 1)
        for start in range(0, block.shape[1], LANES)
    ]
    return jnp.concatenate(pieces, axis=1)


def payload_kernel(
    core_ref, x_ref, tau_ref, classes_ref, keep_ref, out_ref, tau_scr, classes_scr, keep_scr, sems
):
    rows, width = out_ref.shape
    count = keep_scr.shape[1]
    pixels = width - count - LANES
    start = pl.multiple_of(core_ref[0] * pixels, pixels)
    copies = [
        pltpu.make_async_copy(
            x_ref.at[:, pl.ds(start, pixels)], out_ref.at[:, pl.ds(0, pixels)], sems.at[0]
        ),
        pltpu.make_async_copy(tau_ref, tau_scr, sems.at[1]),
        pltpu.make_async_copy(classes_ref, classes_scr, sems.at[2]),
        pltpu.make_async_copy(keep_ref, keep_scr, sems.at[3]),
    ]
    for copy in copies:
        copy.start()
    for copy in copies[1:]:
        copy.wait()
    keep = keep_scr[...].astype(jnp.float32).astype(jnp.bfloat16)
    out_ref[:, pixels : pixels + count] = keep
    eye = lax.broadcasted_iota(jnp.int32, (rows, rows), 0) == lax.broadcasted_iota(
        jnp.int32, (rows, rows), 1
    )
    tau = jnp.sum(
        jnp.where(eye, tau_scr[...].astype(jnp.float32), 0.0), axis=1, keepdims=True
    )
    lane = lax.broadcasted_iota(jnp.int32, (rows, LANES), 1)
    meta = jnp.where(lane == 0, tau, 0.0)
    for j in range(classes_scr.shape[0]):
        named = classes_scr[j : j + 1, :].astype(jnp.float32)
        named = jnp.sum(jnp.where(eye, named, 0.0), axis=1, keepdims=True)
        meta = jnp.where(lane == 1 + j, named, meta)
    out_ref[:, pixels + count :] = meta.astype(jnp.bfloat16)
    copies[0].wait()


def make_payload(core, particles, tau, candidates, prune, pixels):
    rows, choose = candidates.shape
    count = prune.shape[1]
    width = pixels + count + LANES
    return pl.pallas_call(
        payload_kernel,
        in_specs=[pl.BlockSpec(memory_space=pltpu.SMEM)] + [IN_HBM] * 4,
        out_specs=IN_VMEM,
        out_shape=jax.ShapeDtypeStruct((rows, width), jnp.bfloat16),
        scratch_shapes=[
            pltpu.VMEM((1, rows), jnp.bfloat16),
            pltpu.VMEM((choose, rows), jnp.int32),
            pltpu.VMEM((rows, count), jnp.int32),
            pltpu.SemaphoreType.DMA((4,)),
        ],
        compiler_params=pltpu.CompilerParams(vmem_limit_bytes=VMEM_LIMIT),
        name="make_payload",
    )(core, *(in_hbm(x) for x in (particles, tau.reshape(1, rows), candidates.T, prune)))


def pack_kernel(place_ref, x_ref, *out_refs, classes, cap, choose):
    *piece_refs, choice_ref = out_refs
    rows, width = x_ref.shape
    slots = classes * cap
    meta = x_ref[:, width - LANES :].astype(jnp.float32)
    base, flip = place_ref[0], place_ref[1]
    ids = base + (lax.broadcasted_iota(jnp.int32, (rows, classes), 1) ^ flip)
    ids = ids.astype(jnp.float32)
    named = jnp.zeros((rows, classes), jnp.float32)
    for j in range(choose):
        named = jnp.where(meta[:, 1 + j : 2 + j] == ids, 1.0, named)
    earlier = (
        lax.broadcasted_iota(jnp.int32, (rows, rows), 0)
        > lax.broadcasted_iota(jnp.int32, (rows, rows), 1)
    ).astype(jnp.float32)
    rank = jnp.dot(earlier, named, preferred_element_type=jnp.float32)
    slot = lax.broadcasted_iota(jnp.int32, (classes, slots), 1)
    first = lax.broadcasted_iota(jnp.int32, (classes, slots), 0) * cap
    spread = ((slot >= first) & (slot < first + cap)).astype(jnp.float32)
    rank_at = jnp.dot(rank, spread, preferred_element_type=jnp.float32)
    named_at = jnp.dot(named, spread, preferred_element_type=jnp.float32)
    place = (lax.broadcasted_iota(jnp.int32, (rows, slots), 1) % cap).astype(jnp.float32)
    choice = jnp.where((named_at > 0.5) & (rank_at == place), 1.0, 0.0)
    choice_ref[...] = choice
    picks = choice.astype(jnp.bfloat16)
    tile = 11 * LANES
    length = slots // len(piece_refs)
    for start in range(0, width, tile):
        stop = min(start + tile, width)
        packed = lax.dot_general(
            picks,
            x_ref[:, start:stop],
            (((0,), (0,)), ((), ())),
            preferred_element_type=jnp.float32,
        ).astype(jnp.bfloat16)
        for index, piece_ref in enumerate(piece_refs):
            piece_ref[:, start:stop] = packed[index * length : (index + 1) * length]


def pack(place, payload, classes, cap, choose):
    rows, width = payload.shape
    slots = classes * cap
    pieces = piece_count(classes)
    outs = [jax.ShapeDtypeStruct((slots // pieces, width), jnp.bfloat16)] * pieces
    outs.append(jax.ShapeDtypeStruct((rows, slots), jnp.float32))
    *packed, choice = pl.pallas_call(
        functools.partial(pack_kernel, classes=classes, cap=cap, choose=choose),
        in_specs=[pl.BlockSpec(memory_space=pltpu.SMEM), IN_VMEM],
        out_specs=[IN_VMEM] * len(outs),
        out_shape=outs,
        compiler_params=pltpu.CompilerParams(vmem_limit_bytes=VMEM_LIMIT),
        name="pack",
    )(place, payload)
    return packed, choice


def views_kernel(core_ref, mine_ref, theirs_ref, own_ref, other_ref, norm_ref, rest, sems):
    core = core_ref[0]
    _, count, total = mine_ref.shape
    half = total // 2
    images = total // BOX
    before = (core * (images // 2) + images - 1) % images * BOX
    after = (core + 1) * (images // 2) % images * BOX
    copies = []

    def fetch(source_ref, source, target, length):
        source = pl.multiple_of(source, BOX)
        copy = pltpu.make_async_copy(
            source_ref.at[0, :, pl.ds(source, length)], target, sems.at[len(copies)]
        )
        copy.start()
        copies.append(copy)

    for source_ref, out_ref in ((mine_ref, own_ref), (theirs_ref, other_ref)):
        fetch(source_ref, core * half, out_ref.at[:, pl.ds(BOX, half)], half)
        fetch(source_ref, before, out_ref.at[:, pl.ds(0, BOX)], BOX)
        fetch(source_ref, after, out_ref.at[:, pl.ds(BOX + half, BOX)], BOX)
        if source_ref is mine_ref:
            fetch(source_ref, (1 - core) * half, rest, half)
    for copy in copies[:4]:
        copy.wait()
    sums = jnp.zeros((count, LANES), jnp.float32)
    for start in range(0, half, LANES):
        for piece in (own_ref[:, BOX + start : BOX + start + LANES], rest[:, start : start + LANES]):
            piece = piece.astype(jnp.float32)
            sums = sums + piece * piece
    norm_ref[...] = column_to_row(jnp.sum(sums, axis=1, keepdims=True), count)
    for copy in copies[4:]:
        copy.wait()


def make_views(core, mine, theirs):
    _, count, total = mine.shape
    ext = jax.ShapeDtypeStruct((count, total // 2 + 2 * BOX), jnp.bfloat16)
    return pl.pallas_call(
        views_kernel,
        in_specs=[pl.BlockSpec(memory_space=pltpu.SMEM), IN_HBM, IN_HBM],
        out_specs=[IN_VMEM, IN_VMEM, IN_VMEM],
        out_shape=[ext, ext, jax.ShapeDtypeStruct((1, count), jnp.float32)],
        scratch_shapes=[
            pltpu.VMEM((count, total // 2), jnp.bfloat16),
            pltpu.SemaphoreType.DMA((7,)),
        ],
        compiler_params=pltpu.CompilerParams(vmem_limit_bytes=VMEM_LIMIT),
        name="make_views",
    )(core, in_hbm(mine), in_hbm(theirs))


def score_kernel(*refs, pixels):
    *x_refs, own_ref, other_ref, norm_ref, out_ref = refs
    rows = sum(ref.shape[0] for ref in x_refs)
    count = own_ref.shape[0]
    span = 2 * count
    tile = 16 * LANES
    one = jnp.zeros((rows, LANES), jnp.bfloat16)
    two = jnp.zeros((rows, 2 * LANES), jnp.bfloat16)
    total = None
    for start in range(0, pixels, tile):
        image = joined(x_refs, start, start + tile)
        stack = [
            [one, image, one],
            [image, two],
            [two, image],
            [one, roll_lanes(image, -1), one],
            [one, roll_lanes(image, 1), one],
        ]
        stack = jnp.concatenate([jnp.concatenate(line, axis=1) for line in stack], axis=0)
        stop = start + tile + 2 * LANES
        both = jnp.concatenate([own_ref[:, start:stop], other_ref[:, start:stop]], axis=0)
        part = lax.dot_general(
            stack, both, (((1,), (1,)), ((), ())), preferred_element_type=jnp.float32
        )
        total = part if total is None else total + part
    keep = joined(x_refs, pixels, pixels + count).astype(jnp.float32)
    offset = jnp.where(keep > 0.5, 0.0, NEG) - 0.5 * norm_ref[...]
    offset = jnp.concatenate([offset, jnp.zeros_like(offset)], axis=1)
    for index in range(shift_count):
        out_ref[:, index * span : (index + 1) * span] = (
            total[index * rows : (index + 1) * rows] + offset
        )


def half_scores(records, own, other, norms, pixels):
    rows = sum(piece.shape[0] for piece in records)
    count = own.shape[0]
    return pl.pallas_call(
        functools.partial(score_kernel, pixels=pixels),
        in_specs=[IN_VMEM] * (len(records) + 3),
        out_specs=IN_VMEM,
        out_shape=jax.ShapeDtypeStruct((rows, 2 * shift_count * count), jnp.float32),
        compiler_params=pltpu.CompilerParams(vmem_limit_bytes=VMEM_LIMIT),
        name="half_scores",
    )(*records, own, other, norms)


def mean_kernel(mine_ref, theirs_ref, *refs, pixels, pieces):
    x_refs = refs[:pieces]
    own_ref, other_ref = refs[pieces : pieces + 2]
    out_refs = refs[pieces + 2 : 2 * pieces + 2]
    weight_scr = refs[-1]
    length, width = x_refs[0].shape
    rows = length * pieces
    count = own_ref.shape[0]
    span = 2 * count
    tau = joined(x_refs, width - LANES, width)[:, 0:1].astype(jnp.float32)
    scores = []
    peak = jnp.full((rows, 1), NEG, jnp.float32)
    for index in range(shift_count):
        mine = mine_ref[:, index * span : (index + 1) * span]
        theirs = theirs_ref[:, index * span : (index + 1) * span]
        swapped = jnp.concatenate([theirs[:, count:], theirs[:, :count]], axis=1)
        full = mine + swapped
        score = jnp.where(full > -1e29, tau * full, NEG)
        scores.append(score)
        peak = jnp.maximum(peak, jnp.max(score, axis=1, keepdims=True))
    total = jnp.zeros((rows, 1), jnp.float32)
    for index, score in enumerate(scores):
        weight = jnp.where(score > -1e28, jnp.exp(score - peak), 0.0).astype(jnp.bfloat16)
        total = total + jnp.sum(weight.astype(jnp.float32), axis=1, keepdims=True)
        weight_scr[index * rows : (index + 1) * rows, :] = weight
    filled = total > 0
    safe = jnp.where(filled, total, 1.0)
    inverse = 1.0 / safe
    logs = put_log(jnp.where(filled, peak + jnp.log(safe), NEG), rows)
    for index, out_ref in enumerate(out_refs):
        out_ref[:, pixels:] = logs[index * length : (index + 1) * length]

    weights = weight_scr[...]
    tile = 16 * LANES
    for start in range(0, pixels, tile):
        stop = start + tile + 2 * LANES
        both = jnp.concatenate([own_ref[:, start:stop], other_ref[:, start:stop]], axis=0)
        sums = jnp.dot(weights, both, preferred_element_type=jnp.float32)
        inner = slice(LANES, LANES + tile)
        mean = sums[0:rows, inner] + sums[rows : 2 * rows, 0:tile]
        mean = mean + sums[2 * rows : 3 * rows, 2 * LANES : 2 * LANES + tile]
        mean = mean + roll_lanes(sums[3 * rows : 4 * rows, inner], 1)
        mean = mean + roll_lanes(sums[4 * rows : 5 * rows, inner], -1)
        mean = (mean * inverse).astype(jnp.bfloat16)
        for index, out_ref in enumerate(out_refs):
            out_ref[:, start : start + tile] = mean[index * length : (index + 1) * length]


def weighted_means(mine, theirs, records, own, other, pixels):
    length = records[0].shape[0]
    pieces = len(records)
    count = own.shape[0]
    return pl.pallas_call(
        functools.partial(mean_kernel, pixels=pixels, pieces=pieces),
        in_specs=[IN_VMEM] * (pieces + 4),
        out_specs=[IN_VMEM] * pieces,
        out_shape=[jax.ShapeDtypeStruct((length, pixels + LANES), jnp.bfloat16)] * pieces,
        scratch_shapes=[pltpu.VMEM((shift_count * pieces * length, 2 * count), jnp.bfloat16)],
        compiler_params=pltpu.CompilerParams(vmem_limit_bytes=VMEM_LIMIT),
        name="weighted_means",
    )(mine, theirs, *records, own, other)


def mix_kernel(*refs, dense, pixels):
    choice_ref, *back_refs, out_ref = refs
    if dense:
        *back_refs, part_ref = back_refs
    rows, slots = choice_ref.shape
    chosen = choice_ref[...] > 0.5
    row = column_to_row(get_log(joined(back_refs, pixels, pixels + LANES)), slots)
    value = jnp.where(chosen, row, NEG)
    best = jnp.max(value, axis=1, keepdims=True)
    if dense:
        part = get_log(part_ref[:, pixels:])
        best = jnp.maximum(best, part)
    factor = jnp.where(chosen, jnp.exp(value - best), 0.0)
    total = jnp.sum(factor, axis=1, keepdims=True)
    if dense:
        part_factor = jnp.where(part > -1e29, jnp.exp(part - best), 0.0)
        total = total + part_factor
    filled = total > 0
    safe = jnp.where(filled, total, 1.0)
    mixer = jnp.concatenate(split3(factor / safe), axis=0)
    tile = 16 * LANES
    for start in range(0, pixels, tile):
        span = slice(start, start + tile)
        images = joined(back_refs, start, start + tile)
        mixed = jnp.dot(mixer, images, preferred_element_type=jnp.float32)
        mixed = mixed[0:rows] + (mixed[rows : 2 * rows] + mixed[2 * rows : 3 * rows])
        if dense:
            mixed = mixed + (part_factor / safe) * part_ref[:, span].astype(jnp.float32)
        out_ref[:, span] = mixed.astype(jnp.bfloat16)
    if not dense:
        out_ref[:, pixels:] = put_log(jnp.where(filled, best + jnp.log(safe), NEG), rows)


def mix(choice, back, part, pixels):
    rows = choice.shape[0]
    dense = part is not None
    args = [choice, *back, part] if dense else [choice, *back]
    width = pixels if dense else pixels + LANES
    return pl.pallas_call(
        functools.partial(mix_kernel, dense=dense, pixels=pixels),
        in_specs=[IN_VMEM] * len(args),
        out_specs=IN_VMEM,
        out_shape=jax.ShapeDtypeStruct((rows, width), jnp.bfloat16),
        compiler_params=pltpu.CompilerParams(vmem_limit_bytes=VMEM_LIMIT),
        name="mix_final" if dense else "mix_half",
    )(*args)


def trade(pieces, peers):
    if len(pieces) == peers:
        return [pieces[0]] + [
            lax.ppermute(pieces[flip], "lo", [(i, i ^ flip) for i in range(peers)])
            for flip in range(1, peers)
        ]
    whole = pieces[0]
    parts = whole.reshape(peers, whole.shape[0] // peers, whole.shape[1])
    parts = lax.all_to_all(parts, "lo", split_axis=0, concat_axis=0, tiled=True)
    return [parts.reshape(whole.shape)]


def on_device(particles, tau, candidates, prune, projections):
    halves = lax.axis_size("hi")
    peers = lax.axis_size("lo")
    cores = lax.axis_size("ori")
    core = lax.axis_index("ori")
    part_rows, choose = candidates.shape
    pixels = particles.shape[1] // cores
    count = prune.shape[1]
    cap = 2 * part_rows * choose // (halves * peers)
    lo = lax.axis_index("lo").astype(jnp.int32)
    base = lax.axis_index("hi").astype(jnp.int32) * peers
    place = jnp.stack([base, lo if piece_count(peers) == peers else jnp.zeros_like(lo)])
    across = [(i, (i + 1) % halves) for i in range(halves)]
    swap = [(i, (i + 1) % cores) for i in range(cores)]

    core_id = core.astype(jnp.int32).reshape(1)
    payload = make_payload(core_id, particles, tau, candidates, prune, pixels)
    far_payload = lax.ppermute(payload, "hi", across)

    sent_near, choice_near = pack(place, payload, peers, cap, choose)
    records_near = trade(sent_near, peers)

    other = lax.ppermute(projections, "ori", swap)
    own_views, other_views, norms = make_views(core_id, projections, other)

    sent_far, choice_far = pack(place, far_payload, peers, cap, choose)
    sent_far, records_near = lax.optimization_barrier((sent_far, records_near))
    records_far = trade(sent_far, peers)

    def scores(records):
        mine = half_scores(records, own_views, other_views, norms, pixels)
        return mine, lax.ppermute(mine, "ori", swap)

    def means(sums, records):
        return weighted_means(*sums, records, own_views, other_views, pixels)

    far_means = means(scores(records_far), records_far)
    back_far = trade(far_means, peers)

    records_near, far_means = lax.optimization_barrier((records_near, far_means))
    near_means = means(scores(records_near), records_near)
    near_means, back_far = lax.optimization_barrier((near_means, back_far))

    far_mix = mix(choice_far, back_far, None, pixels)
    part_mix = lax.ppermute(far_mix, "hi", across)
    back_near = trade(near_means, peers)
    return mix(choice_near, back_near, part_mix, pixels)


def solution(mesh):
    grp, cls, ori = (mesh.shape[name] for name in ("grp", "cls", "ori"))
    inner = Mesh(mesh.devices.reshape(grp, 2, cls // 2, ori), ("grp", "hi", "lo", "ori"))
    rows = ("grp", "hi", "lo")
    placed = (
        P(rows, None),
        P(rows),
        P(rows, None),
        P(rows, "ori"),
        P(("hi", "lo"), "ori", None),
    )
    return jax.shard_map(
        on_device, mesh=inner, in_specs=placed, out_specs=P(rows, "ori"), check_vma=False
    )
```

```python
import functools

import jax
import jax.numpy as jnp
from jax import lax
from jax.experimental import pallas as pl
from jax.experimental.pallas import tpu as pltpu
from jax.sharding import Mesh
from jax.sharding import PartitionSpec as P

BOX = 128
LANES = 128
NEG = -1e30
shift_count = 5
GIVEN_SHARE = 4
VMEM_LIMIT = 24 * 1024 * 1024
IN_HBM = pl.BlockSpec(memory_space=pltpu.HBM)
IN_VMEM = pl.BlockSpec(memory_space=pltpu.VMEM)


def in_hbm(array):
    return pltpu.with_memory_space_constraint(array, pltpu.HBM)


def joined(refs, start, stop):
    if len(refs) == 1:
        return refs[0][:, start:stop]
    return jnp.concatenate([ref[:, start:stop] for ref in refs], axis=0)


def tiles_of(spans):
    tile = 16 * LANES
    for place, start, length in spans:
        for offset in range(0, length, tile):
            yield place + offset, start + offset, min(tile, length - offset)


def cut(pixels, *shares):
    ends = [pixels // 8 * share for share in shares] + [pixels]
    return tuple(zip([0] + ends[:-1], ends))


def piece_count(peers):
    return peers if peers <= 4 else 1


def split3(value):
    high = value.astype(jnp.bfloat16)
    rest = value - high.astype(jnp.float32)
    middle = rest.astype(jnp.bfloat16)
    low = (rest - middle.astype(jnp.float32)).astype(jnp.bfloat16)
    return high, middle, low


def put_log(value, rows):
    high, middle, low = split3(value)
    lane = lax.broadcasted_iota(jnp.int32, (rows, LANES), 1)
    pieces = jnp.where(
        lane == 0,
        high.astype(jnp.float32),
        jnp.where(
            lane == 1,
            middle.astype(jnp.float32),
            jnp.where(lane == 2, low.astype(jnp.float32), 0.0),
        ),
    )
    return pieces.astype(jnp.bfloat16)


def get_log(pieces):
    wide = pieces.astype(jnp.float32)
    return (wide[:, 0:1] + wide[:, 1:2]) + wide[:, 2:3]


def column_to_row(column, count):
    eye = lax.broadcasted_iota(jnp.int32, (count, count), 0) == lax.broadcasted_iota(
        jnp.int32, (count, count), 1
    )
    return jnp.sum(jnp.where(eye, column, 0.0), axis=0, keepdims=True)


def roll_lanes(block, amount):
    pieces = [
        pltpu.roll(block[:, start : start + LANES], amount % LANES, 1)
        for start in range(0, block.shape[1], LANES)
    ]
    return jnp.concatenate(pieces, axis=1)


def payload_kernel(
    core_ref, x_ref, tau_ref, classes_ref, keep_ref, *refs, chunks
):
    out_refs = refs[: len(chunks)]
    tau_scr, classes_scr, keep_scr, sems = refs[len(chunks) :]
    first_ref = out_refs[0]
    rows = first_ref.shape[0]
    count = keep_scr.shape[1]
    pixels = chunks[-1][1]
    copies = [
        pltpu.make_async_copy(tau_ref, tau_scr, sems.at[0]),
        pltpu.make_async_copy(classes_ref, classes_scr, sems.at[1]),
        pltpu.make_async_copy(keep_ref, keep_scr, sems.at[2]),
    ]
    for out_ref, (start, stop) in zip(out_refs, chunks):
        source = pl.multiple_of(core_ref[0] * pixels + start, LANES)
        copies.append(
            pltpu.make_async_copy(
                x_ref.at[:, pl.ds(source, stop - start)],
                out_ref.at[:, pl.ds(0, stop - start)],
                sems.at[len(copies)],
            )
        )
    for copy in copies:
        copy.start()
    for copy in copies[:3]:
        copy.wait()
    end = chunks[0][1]
    keep = keep_scr[...].astype(jnp.float32).astype(jnp.bfloat16)
    first_ref[:, end : end + count] = keep
    eye = lax.broadcasted_iota(jnp.int32, (rows, rows), 0) == lax.broadcasted_iota(
        jnp.int32, (rows, rows), 1
    )
    tau = jnp.sum(
        jnp.where(eye, tau_scr[...].astype(jnp.float32), 0.0), axis=1, keepdims=True
    )
    lane = lax.broadcasted_iota(jnp.int32, (rows, LANES), 1)
    meta = jnp.where(lane == 0, tau, 0.0)
    for j in range(classes_scr.shape[0]):
        named = classes_scr[j : j + 1, :].astype(jnp.float32)
        named = jnp.sum(jnp.where(eye, named, 0.0), axis=1, keepdims=True)
        meta = jnp.where(lane == 1 + j, named, meta)
    first_ref[:, end + count :] = meta.astype(jnp.bfloat16)
    for copy in copies[3:]:
        copy.wait()


def make_payload(core, particles, tau, candidates, prune, chunks):
    rows, choose = candidates.shape
    count = prune.shape[1]
    widths = [stop - start for start, stop in chunks]
    widths[0] += count + LANES
    return pl.pallas_call(
        functools.partial(payload_kernel, chunks=chunks),
        in_specs=[pl.BlockSpec(memory_space=pltpu.SMEM)] + [IN_HBM] * 4,
        out_specs=[IN_VMEM] * len(chunks),
        out_shape=[jax.ShapeDtypeStruct((rows, width), jnp.bfloat16) for width in widths],
        scratch_shapes=[
            pltpu.VMEM((1, rows), jnp.bfloat16),
            pltpu.VMEM((choose, rows), jnp.int32),
            pltpu.VMEM((rows, count), jnp.int32),
            pltpu.SemaphoreType.DMA((3 + len(chunks),)),
        ],
        compiler_params=pltpu.CompilerParams(vmem_limit_bytes=VMEM_LIMIT),
        name="make_payload",
    )(core, *(in_hbm(x) for x in (particles, tau.reshape(1, rows), candidates.T, prune)))


def choose_slots(meta, base, flip, classes, cap, choose):
    rows = meta.shape[0]
    slots = classes * cap
    ids = base + (lax.broadcasted_iota(jnp.int32, (rows, classes), 1) ^ flip)
    ids = ids.astype(jnp.float32)
    named = jnp.zeros((rows, classes), jnp.float32)
    for j in range(choose):
        named = jnp.where(meta[:, 1 + j : 2 + j] == ids, 1.0, named)
    earlier = (
        lax.broadcasted_iota(jnp.int32, (rows, rows), 0)
        > lax.broadcasted_iota(jnp.int32, (rows, rows), 1)
    ).astype(jnp.float32)
    rank = jnp.dot(earlier, named, preferred_element_type=jnp.float32)
    slot = lax.broadcasted_iota(jnp.int32, (classes, slots), 1)
    first = lax.broadcasted_iota(jnp.int32, (classes, slots), 0) * cap
    spread = ((slot >= first) & (slot < first + cap)).astype(jnp.float32)
    rank_at = jnp.dot(rank, spread, preferred_element_type=jnp.float32)
    named_at = jnp.dot(named, spread, preferred_element_type=jnp.float32)
    place = (lax.broadcasted_iota(jnp.int32, (rows, slots), 1) % cap).astype(jnp.float32)
    return jnp.where((named_at > 0.5) & (rank_at == place), 1.0, 0.0)


def pack_kernel(place_ref, *refs, sources, classes, cap, choose, known):
    x_refs = refs[:sources]
    if known:
        choice_ref = refs[sources]
        piece_refs = refs[sources + 1 :]
        choice = choice_ref[...]
    else:
        *piece_refs, choice_ref = refs[sources:]
        width = x_refs[0].shape[1]
        meta = x_refs[0][:, width - LANES :].astype(jnp.float32)
        choice = choose_slots(meta, place_ref[0], place_ref[1], classes, cap, choose)
        choice_ref[...] = choice
    picks = choice.astype(jnp.bfloat16)
    length = classes * cap // len(piece_refs)
    place = 0
    tile = 16 * LANES
    for x_ref in reversed(x_refs):
        width = x_ref.shape[1]
        for start in range(0, width, tile):
            stop = min(start + tile, width)
            packed = lax.dot_general(
                picks,
                x_ref[:, start:stop],
                (((0,), (0,)), ((), ())),
                preferred_element_type=jnp.float32,
            ).astype(jnp.bfloat16)
            for index, piece_ref in enumerate(piece_refs):
                piece_ref[:, place + start : place + stop] = packed[
                    index * length : (index + 1) * length
                ]
        place += width


def pack(place, chunks, pieces, classes, cap, choose, choice=None):
    rows = chunks[0].shape[0]
    width = sum(chunk.shape[1] for chunk in chunks)
    slots = classes * cap
    known = choice is not None
    outs = [jax.ShapeDtypeStruct((slots // pieces, width), jnp.bfloat16)] * pieces
    if not known:
        outs.append(jax.ShapeDtypeStruct((rows, slots), jnp.float32))
    args = [*chunks, choice] if known else chunks
    packed = pl.pallas_call(
        functools.partial(
            pack_kernel,
            sources=len(chunks),
            classes=classes,
            cap=cap,
            choose=choose,
            known=known,
        ),
        in_specs=[pl.BlockSpec(memory_space=pltpu.SMEM)] + [IN_VMEM] * len(args),
        out_specs=[IN_VMEM] * len(outs),
        out_shape=outs,
        compiler_params=pltpu.CompilerParams(vmem_limit_bytes=VMEM_LIMIT),
        name="pack_rest" if known else "pack",
    )(place, *args)
    return packed if known else (packed[:-1], packed[-1])


def views_kernel(core_ref, mine_ref, theirs_ref, own_ref, other_ref, norm_ref, rest, sems):
    core = core_ref[0]
    _, count, total = mine_ref.shape
    half = total // 2
    images = total // BOX
    before = (core * (images // 2) + images - 1) % images * BOX
    after = (core + 1) * (images // 2) % images * BOX
    copies = []

    def fetch(source_ref, source, target, length):
        source = pl.multiple_of(source, BOX)
        copy = pltpu.make_async_copy(
            source_ref.at[0, :, pl.ds(source, length)], target, sems.at[len(copies)]
        )
        copy.start()
        copies.append(copy)

    for source_ref, out_ref in ((mine_ref, own_ref), (theirs_ref, other_ref)):
        fetch(source_ref, core * half, out_ref.at[:, pl.ds(BOX, half)], half)
        fetch(source_ref, before, out_ref.at[:, pl.ds(0, BOX)], BOX)
        fetch(source_ref, after, out_ref.at[:, pl.ds(BOX + half, BOX)], BOX)
        if source_ref is mine_ref:
            fetch(source_ref, (1 - core) * half, rest, half)
    for copy in copies[:4]:
        copy.wait()
    sums = jnp.zeros((count, LANES), jnp.float32)
    for start in range(0, half, LANES):
        for piece in (own_ref[:, BOX + start : BOX + start + LANES], rest[:, start : start + LANES]):
            piece = piece.astype(jnp.float32)
            sums = sums + piece * piece
    norm_ref[...] = column_to_row(jnp.sum(sums, axis=1, keepdims=True), count)
    for copy in copies[4:]:
        copy.wait()


def make_views(core, mine, theirs):
    _, count, total = mine.shape
    ext = jax.ShapeDtypeStruct((count, total // 2 + 2 * BOX), jnp.bfloat16)
    return pl.pallas_call(
        views_kernel,
        in_specs=[pl.BlockSpec(memory_space=pltpu.SMEM), IN_HBM, IN_HBM],
        out_specs=[IN_VMEM, IN_VMEM, IN_VMEM],
        out_shape=[ext, ext, jax.ShapeDtypeStruct((1, count), jnp.float32)],
        scratch_shapes=[
            pltpu.VMEM((count, total // 2), jnp.bfloat16),
            pltpu.SemaphoreType.DMA((7,)),
        ],
        compiler_params=pltpu.CompilerParams(vmem_limit_bytes=VMEM_LIMIT),
        name="make_views",
    )(core, in_hbm(mine), in_hbm(theirs))


def score_kernel(*refs, pieces, spans, masked, added):
    x_refs = refs[:pieces]
    own_ref, other_ref, norm_ref = refs[pieces : pieces + 3]
    out_ref = refs[-1]
    rows = sum(ref.shape[0] for ref in x_refs)
    count = own_ref.shape[0]
    span = 2 * count
    one = jnp.zeros((rows, LANES), jnp.bfloat16)
    two = jnp.zeros((rows, 2 * LANES), jnp.bfloat16)
    total = None
    for place, start, tile in tiles_of(spans):
        image = joined(x_refs, place, place + tile)
        stack = [
            [one, image, one],
            [image, two],
            [two, image],
            [one, roll_lanes(image, -1), one],
            [one, roll_lanes(image, 1), one],
        ]
        stack = jnp.concatenate([jnp.concatenate(line, axis=1) for line in stack], axis=0)
        stop = start + tile + 2 * LANES
        both = jnp.concatenate([own_ref[:, start:stop], other_ref[:, start:stop]], axis=0)
        part = lax.dot_general(
            stack, both, (((1,), (1,)), ((), ())), preferred_element_type=jnp.float32
        )
        total = part if total is None else total + part
    if masked:
        width = x_refs[0].shape[1]
        keep = joined(x_refs, width - LANES - count, width - LANES).astype(jnp.float32)
        offset = jnp.where(keep > 0.5, 0.0, NEG) - 0.5 * norm_ref[...]
        offset = jnp.concatenate([offset, jnp.zeros_like(offset)], axis=1)
    for index in range(shift_count):
        block = slice(index * span, (index + 1) * span)
        value = total[index * rows : (index + 1) * rows]
        if masked:
            value = value + offset
        if added:
            value = value + refs[pieces + 3][:, block]
        out_ref[:, block] = value


def half_scores(records, own, other, norms, spans, masked, earlier=None):
    rows = sum(piece.shape[0] for piece in records)
    count = own.shape[0]
    args = [*records, own, other, norms]
    if earlier is not None:
        args.append(earlier)
    return pl.pallas_call(
        functools.partial(
            score_kernel,
            pieces=len(records),
            spans=spans,
            masked=masked,
            added=earlier is not None,
        ),
        in_specs=[IN_VMEM] * len(args),
        out_specs=IN_VMEM,
        out_shape=jax.ShapeDtypeStruct((rows, 2 * shift_count * count), jnp.float32),
        compiler_params=pltpu.CompilerParams(vmem_limit_bytes=VMEM_LIMIT),
        name="half_scores",
    )(*args)


def weigh(mine_ref, theirs_ref, tau, count, weight_ref):
    rows = tau.shape[0]
    span = 2 * count
    scores = []
    peak = jnp.full((rows, 1), NEG, jnp.float32)
    for index in range(shift_count):
        mine = mine_ref[:, index * span : (index + 1) * span]
        theirs = theirs_ref[:, index * span : (index + 1) * span]
        swapped = jnp.concatenate([theirs[:, count:], theirs[:, :count]], axis=1)
        full = mine + swapped
        score = jnp.where(full > -1e29, tau * full, NEG)
        scores.append(score)
        peak = jnp.maximum(peak, jnp.max(score, axis=1, keepdims=True))
    total = jnp.zeros((rows, 1), jnp.float32)
    for index, score in enumerate(scores):
        weight = jnp.where(score > -1e28, jnp.exp(score - peak), 0.0).astype(jnp.bfloat16)
        total = total + jnp.sum(weight.astype(jnp.float32), axis=1, keepdims=True)
        weight_ref[index * rows : (index + 1) * rows, :] = weight
    filled = total > 0
    safe = jnp.where(filled, total, 1.0)
    return 1.0 / safe, put_log(jnp.where(filled, peak + jnp.log(safe), NEG), rows)


def write_means(weight_ref, inverse, own_ref, other_ref, out_refs, start, stop):
    length = out_refs[0].shape[0]
    rows = length * len(out_refs)
    weights = weight_ref[...]
    for place, first, tile in tiles_of([(0, start, stop - start)]):
        end = first + tile + 2 * LANES
        both = jnp.concatenate([own_ref[:, first:end], other_ref[:, first:end]], axis=0)
        sums = jnp.dot(weights, both, preferred_element_type=jnp.float32)
        inner = slice(LANES, LANES + tile)
        mean = sums[0:rows, inner] + sums[rows : 2 * rows, 0:tile]
        mean = mean + sums[2 * rows : 3 * rows, 2 * LANES : 2 * LANES + tile]
        mean = mean + roll_lanes(sums[3 * rows : 4 * rows, inner], 1)
        mean = mean + roll_lanes(sums[4 * rows : 5 * rows, inner], -1)
        mean = (mean * inverse).astype(jnp.bfloat16)
        for index, out_ref in enumerate(out_refs):
            out_ref[:, place : place + tile] = mean[index * length : (index + 1) * length]


def mean_kernel(mine_ref, theirs_ref, *refs, chunk, pieces):
    x_refs = refs[:pieces]
    own_ref, other_ref = refs[pieces : pieces + 2]
    out_refs = refs[pieces + 2 : 2 * pieces + 2]
    weight_ref, inverse_ref = refs[2 * pieces + 2 :]
    length, width = x_refs[0].shape
    tau = joined(x_refs, width - LANES, width)[:, 0:1].astype(jnp.float32)
    inverse, logs = weigh(mine_ref, theirs_ref, tau, own_ref.shape[0], weight_ref)
    inverse_ref[...] = jnp.broadcast_to(inverse, inverse_ref.shape)
    start, stop = chunk
    for index, out_ref in enumerate(out_refs):
        out_ref[:, stop - start :] = logs[index * length : (index + 1) * length]
    write_means(weight_ref, inverse, own_ref, other_ref, out_refs, start, stop)


def weighted_means(mine, theirs, records, own, other, chunk):
    length = records[0].shape[0]
    pieces = len(records)
    count = own.shape[0]
    outs = [jax.ShapeDtypeStruct((length, chunk[1] - chunk[0] + LANES), jnp.bfloat16)] * pieces
    outs += [
        jax.ShapeDtypeStruct((shift_count * pieces * length, 2 * count), jnp.bfloat16),
        jax.ShapeDtypeStruct((pieces * length, LANES), jnp.float32),
    ]
    *means, weights, inverse = pl.pallas_call(
        functools.partial(mean_kernel, chunk=chunk, pieces=pieces),
        in_specs=[IN_VMEM] * (pieces + 4),
        out_specs=[IN_VMEM] * len(outs),
        out_shape=outs,
        compiler_params=pltpu.CompilerParams(vmem_limit_bytes=VMEM_LIMIT),
        name="weighted_means",
    )(mine, theirs, *records, own, other)
    return means, weights, inverse


def rest_kernel(weight_ref, inverse_ref, own_ref, other_ref, *out_refs, chunk):
    write_means(weight_ref, inverse_ref[:, 0:1], own_ref, other_ref, out_refs, *chunk)


def rest_of_means(weights, inverse, own, other, chunk, pieces):
    length = inverse.shape[0] // pieces
    return pl.pallas_call(
        functools.partial(rest_kernel, chunk=chunk),
        in_specs=[IN_VMEM] * 4,
        out_specs=[IN_VMEM] * pieces,
        out_shape=[jax.ShapeDtypeStruct((length, chunk[1] - chunk[0]), jnp.bfloat16)] * pieces,
        compiler_params=pltpu.CompilerParams(vmem_limit_bytes=VMEM_LIMIT),
        name="rest_of_means",
    )(weights, inverse, own, other)


def half_mix_kernel(choice_ref, *refs, pieces):
    back_refs = refs[:pieces]
    out_ref, mixer_ref = refs[pieces:]
    rows, slots = choice_ref.shape
    width = out_ref.shape[1] - LANES
    chosen = choice_ref[...] > 0.5
    row = column_to_row(get_log(joined(back_refs, width, width + LANES)), slots)
    value = jnp.where(chosen, row, NEG)
    best = jnp.max(value, axis=1, keepdims=True)
    factor = jnp.where(chosen, jnp.exp(value - best), 0.0)
    total = jnp.sum(factor, axis=1, keepdims=True)
    filled = total > 0
    safe = jnp.where(filled, total, 1.0)
    mixer = jnp.concatenate(split3(factor / safe), axis=0)
    mixer_ref[...] = mixer
    out_ref[:, width:] = put_log(jnp.where(filled, best + jnp.log(safe), NEG), rows)
    write_mix(mixer, back_refs, out_ref, width)


def write_mix(mixer, back_refs, out_ref, width):
    rows = out_ref.shape[0]
    for place, _, tile in tiles_of([(0, 0, width)]):
        images = joined(back_refs, place, place + tile)
        mixed = jnp.dot(mixer, images, preferred_element_type=jnp.float32)
        mixed = mixed[0:rows] + (mixed[rows : 2 * rows] + mixed[2 * rows : 3 * rows])
        out_ref[:, place : place + tile] = mixed.astype(jnp.bfloat16)


def rest_mix_kernel(mixer_ref, *refs):
    *back_refs, out_ref = refs
    write_mix(mixer_ref[...], back_refs, out_ref, out_ref.shape[1])


def half_mix(choice, back):
    rows, slots = choice.shape
    return pl.pallas_call(
        functools.partial(half_mix_kernel, pieces=len(back)),
        in_specs=[IN_VMEM] * (1 + len(back)),
        out_specs=[IN_VMEM] * 2,
        out_shape=[
            jax.ShapeDtypeStruct((rows, back[0].shape[1]), jnp.bfloat16),
            jax.ShapeDtypeStruct((3 * rows, slots), jnp.bfloat16),
        ],
        compiler_params=pltpu.CompilerParams(vmem_limit_bytes=VMEM_LIMIT),
        name="half_mix",
    )(choice, *back)


def rest_of_mix(mixer, back):
    rows = mixer.shape[0] // 3
    return pl.pallas_call(
        rest_mix_kernel,
        in_specs=[IN_VMEM] * (1 + len(back)),
        out_specs=IN_VMEM,
        out_shape=jax.ShapeDtypeStruct((rows, back[0].shape[1]), jnp.bfloat16),
        compiler_params=pltpu.CompilerParams(vmem_limit_bytes=VMEM_LIMIT),
        name="rest_of_mix",
    )(mixer, *back)


def final_kernel(choice_ref, *refs, pieces, chunks):
    back_refs = refs[:pieces]
    part_refs = refs[pieces:-1]
    out_ref = refs[-1]
    rows, slots = choice_ref.shape
    pixels = chunks[-1][1]
    end = chunks[0][1]
    chosen = choice_ref[...] > 0.5
    row = column_to_row(get_log(joined(back_refs, pixels, pixels + LANES)), slots)
    value = jnp.where(chosen, row, NEG)
    part = get_log(part_refs[0][:, end:])
    best = jnp.maximum(jnp.max(value, axis=1, keepdims=True), part)
    factor = jnp.where(chosen, jnp.exp(value - best), 0.0)
    part_factor = jnp.where(part > -1e29, jnp.exp(part - best), 0.0)
    total = jnp.sum(factor, axis=1, keepdims=True) + part_factor
    safe = jnp.where(total > 0, total, 1.0)
    part_factor = part_factor / safe
    mixer = jnp.concatenate(split3(factor / safe), axis=0)
    for (first, last), part_ref in zip(chunks, part_refs):
        for place, start, tile in tiles_of([(0, first, last - first)]):
            images = joined(back_refs, start, start + tile)
            mixed = jnp.dot(mixer, images, preferred_element_type=jnp.float32)
            mixed = mixed[0:rows] + (mixed[rows : 2 * rows] + mixed[2 * rows : 3 * rows])
            mixed = mixed + part_factor * part_ref[:, place : place + tile].astype(jnp.float32)
            out_ref[:, start : start + tile] = mixed.astype(jnp.bfloat16)


def final_mix(choice, back, parts, chunks):
    rows = choice.shape[0]
    args = [choice, *back, *parts]
    return pl.pallas_call(
        functools.partial(final_kernel, pieces=len(back), chunks=chunks),
        in_specs=[IN_VMEM] * len(args),
        out_specs=IN_VMEM,
        out_shape=jax.ShapeDtypeStruct((rows, chunks[-1][1]), jnp.bfloat16),
        compiler_params=pltpu.CompilerParams(vmem_limit_bytes=VMEM_LIMIT),
        name="final_mix",
    )(*args)


def trade(pieces, peers):
    if len(pieces) == peers:
        return [pieces[0]] + [
            lax.ppermute(pieces[flip], "lo", [(i, i ^ flip) for i in range(peers)])
            for flip in range(1, peers)
        ]
    whole = pieces[0]
    parts = whole.reshape(peers, whole.shape[0] // peers, whole.shape[1])
    parts = lax.all_to_all(parts, "lo", split_axis=0, concat_axis=0, tiled=True)
    return [parts.reshape(whole.shape)]


def on_device(particles, tau, candidates, prune, projections):
    halves = lax.axis_size("hi")
    peers = lax.axis_size("lo")
    cores = lax.axis_size("ori")
    core = lax.axis_index("ori")
    part_rows, choose = candidates.shape
    pixels = particles.shape[1] // cores
    count = prune.shape[1]
    cap = 2 * part_rows * choose // (halves * peers)
    lo = lax.axis_index("lo").astype(jnp.int32)
    base = lax.axis_index("hi").astype(jnp.int32) * peers
    pieces = piece_count(peers)
    natural = jnp.stack([base, jnp.zeros_like(lo)])
    place = jnp.stack([base, lo if pieces == peers else jnp.zeros_like(lo)])
    across = [(i, (i + 1) % halves) for i in range(halves)]
    swap = [(i, (i + 1) % cores) for i in range(cores)]

    core_id = core.astype(jnp.int32).reshape(1)
    whole = ((0, pixels),)
    given = cut(pixels, GIVEN_SHARE)
    payload = make_payload(core_id, particles, tau, candidates, prune, whole)
    far_payload = [lax.ppermute(chunk, "hi", across) for chunk in payload]

    sent_near, choice_near = pack(place, payload, pieces, peers, cap, choose)
    records_near = trade(sent_near, peers)

    other = lax.ppermute(projections, "ori", swap)
    own_views, other_views, norms = make_views(core_id, projections, other)
    far_payload, own_views = lax.optimization_barrier((far_payload, own_views))
    views = (own_views, other_views)

    sent_far, choice_far = pack(place, far_payload, pieces, peers, cap, choose)
    sent_far, records_near = lax.optimization_barrier((sent_far, records_near))
    records_far = trade(sent_far, peers)

    spans = ((0, 0, pixels),)
    mine = half_scores(records_far, *views, norms, spans, True)
    theirs = lax.ppermute(mine, "ori", swap)
    far_means, weights, inverse = weighted_means(mine, theirs, records_far, *views, given[0])
    back_far = trade(far_means, peers)
    rest_means = rest_of_means(weights, inverse, *views, given[1], len(far_means))
    back_rest = trade(rest_means, peers)

    records_near, rest_means = lax.optimization_barrier((records_near, rest_means))
    mine = half_scores(records_near, *views, norms, spans, True)
    theirs = lax.ppermute(mine, "ori", swap)
    near_means, _, _ = weighted_means(mine, theirs, records_near, *views, (0, pixels))
    far_mix, mixer = half_mix(choice_far, back_far)
    part_mix = lax.ppermute(far_mix, "hi", across)
    rest_mix = rest_of_mix(mixer, back_rest)
    rest_part = lax.ppermute(rest_mix, "hi", across)
    back_near = trade(near_means, peers)
    return final_mix(choice_near, back_near, (part_mix, rest_part), given)


def solution(mesh):
    grp, cls, ori = (mesh.shape[name] for name in ("grp", "cls", "ori"))
    inner = Mesh(mesh.devices.reshape(grp, 2, cls // 2, ori), ("grp", "hi", "lo", "ori"))
    rows = ("grp", "hi", "lo")
    placed = (
        P(rows, None),
        P(rows),
        P(rows, None),
        P(rows, "ori"),
        P(("hi", "lo"), "ori", None),
    )
    return jax.shard_map(
        on_device, mesh=inner, in_specs=placed, out_specs=P(rows, "ori"), check_vma=False
    )
```

```python
import functools

import jax
import jax.numpy as jnp
from jax import lax
from jax.experimental import pallas as pl
from jax.experimental.pallas import tpu as pltpu
from jax.sharding import Mesh
from jax.sharding import PartitionSpec as P

BOX = 128
LANES = 128
NEG = -1e30
shift_count = 5
GIVEN_SHARE = 4
SENT_SHARE = 4
VMEM_LIMIT = 24 * 1024 * 1024
IN_HBM = pl.BlockSpec(memory_space=pltpu.HBM)
IN_VMEM = pl.BlockSpec(memory_space=pltpu.VMEM)


def in_hbm(array):
    return pltpu.with_memory_space_constraint(array, pltpu.HBM)


def joined(refs, start, stop):
    if len(refs) == 1:
        return refs[0][:, start:stop]
    return jnp.concatenate([ref[:, start:stop] for ref in refs], axis=0)


def tiles_of(spans):
    tile = 16 * LANES
    for place, start, length in spans:
        for offset in range(0, length, tile):
            yield place + offset, start + offset, min(tile, length - offset)


def cut(pixels, *shares):
    ends = [pixels // 8 * share for share in shares] + [pixels]
    return tuple(zip([0] + ends[:-1], ends))


def piece_count(peers):
    return peers if peers <= 4 else 1


def split3(value):
    high = value.astype(jnp.bfloat16)
    rest = value - high.astype(jnp.float32)
    middle = rest.astype(jnp.bfloat16)
    low = (rest - middle.astype(jnp.float32)).astype(jnp.bfloat16)
    return high, middle, low


def put_log(value, rows):
    high, middle, low = split3(value)
    lane = lax.broadcasted_iota(jnp.int32, (rows, LANES), 1)
    pieces = jnp.where(
        lane == 0,
        high.astype(jnp.float32),
        jnp.where(
            lane == 1,
            middle.astype(jnp.float32),
            jnp.where(lane == 2, low.astype(jnp.float32), 0.0),
        ),
    )
    return pieces.astype(jnp.bfloat16)


def get_log(pieces):
    wide = pieces.astype(jnp.float32)
    return (wide[:, 0:1] + wide[:, 1:2]) + wide[:, 2:3]


def column_to_row(column, count):
    eye = lax.broadcasted_iota(jnp.int32, (count, count), 0) == lax.broadcasted_iota(
        jnp.int32, (count, count), 1
    )
    return jnp.sum(jnp.where(eye, column, 0.0), axis=0, keepdims=True)


def roll_lanes(block, amount):
    pieces = [
        pltpu.roll(block[:, start : start + LANES], amount % LANES, 1)
        for start in range(0, block.shape[1], LANES)
    ]
    return jnp.concatenate(pieces, axis=1)


def payload_kernel(
    core_ref, x_ref, tau_ref, classes_ref, keep_ref, *refs, chunks
):
    out_refs = refs[: len(chunks)]
    tau_scr, classes_scr, keep_scr, sems = refs[len(chunks) :]
    first_ref = out_refs[0]
    rows = first_ref.shape[0]
    count = keep_scr.shape[1]
    pixels = chunks[-1][1]
    copies = [
        pltpu.make_async_copy(tau_ref, tau_scr, sems.at[0]),
        pltpu.make_async_copy(classes_ref, classes_scr, sems.at[1]),
        pltpu.make_async_copy(keep_ref, keep_scr, sems.at[2]),
    ]
    for out_ref, (start, stop) in zip(out_refs, chunks):
        source = pl.multiple_of(core_ref[0] * pixels + start, LANES)
        copies.append(
            pltpu.make_async_copy(
                x_ref.at[:, pl.ds(source, stop - start)],
                out_ref.at[:, pl.ds(0, stop - start)],
                sems.at[len(copies)],
            )
        )
    for copy in copies:
        copy.start()
    for copy in copies[:3]:
        copy.wait()
    end = chunks[0][1]
    keep = keep_scr[...].astype(jnp.float32).astype(jnp.bfloat16)
    first_ref[:, end : end + count] = keep
    eye = lax.broadcasted_iota(jnp.int32, (rows, rows), 0) == lax.broadcasted_iota(
        jnp.int32, (rows, rows), 1
    )
    tau = jnp.sum(
        jnp.where(eye, tau_scr[...].astype(jnp.float32), 0.0), axis=1, keepdims=True
    )
    lane = lax.broadcasted_iota(jnp.int32, (rows, LANES), 1)
    meta = jnp.where(lane == 0, tau, 0.0)
    for j in range(classes_scr.shape[0]):
        named = classes_scr[j : j + 1, :].astype(jnp.float32)
        named = jnp.sum(jnp.where(eye, named, 0.0), axis=1, keepdims=True)
        meta = jnp.where(lane == 1 + j, named, meta)
    first_ref[:, end + count :] = meta.astype(jnp.bfloat16)
    for copy in copies[3:]:
        copy.wait()


def make_payload(core, particles, tau, candidates, prune, chunks):
    rows, choose = candidates.shape
    count = prune.shape[1]
    widths = [stop - start for start, stop in chunks]
    widths[0] += count + LANES
    return pl.pallas_call(
        functools.partial(payload_kernel, chunks=chunks),
        in_specs=[pl.BlockSpec(memory_space=pltpu.SMEM)] + [IN_HBM] * 4,
        out_specs=[IN_VMEM] * len(chunks),
        out_shape=[jax.ShapeDtypeStruct((rows, width), jnp.bfloat16) for width in widths],
        scratch_shapes=[
            pltpu.VMEM((1, rows), jnp.bfloat16),
            pltpu.VMEM((choose, rows), jnp.int32),
            pltpu.VMEM((rows, count), jnp.int32),
            pltpu.SemaphoreType.DMA((3 + len(chunks),)),
        ],
        compiler_params=pltpu.CompilerParams(vmem_limit_bytes=VMEM_LIMIT),
        name="make_payload",
    )(core, *(in_hbm(x) for x in (particles, tau.reshape(1, rows), candidates.T, prune)))


def choose_slots(meta, base, flip, classes, cap, choose):
    rows = meta.shape[0]
    slots = classes * cap
    ids = base + (lax.broadcasted_iota(jnp.int32, (rows, classes), 1) ^ flip)
    ids = ids.astype(jnp.float32)
    named = jnp.zeros((rows, classes), jnp.float32)
    for j in range(choose):
        named = jnp.where(meta[:, 1 + j : 2 + j] == ids, 1.0, named)
    earlier = (
        lax.broadcasted_iota(jnp.int32, (rows, rows), 0)
        > lax.broadcasted_iota(jnp.int32, (rows, rows), 1)
    ).astype(jnp.float32)
    rank = jnp.dot(earlier, named, preferred_element_type=jnp.float32)
    slot = lax.broadcasted_iota(jnp.int32, (classes, slots), 1)
    first = lax.broadcasted_iota(jnp.int32, (classes, slots), 0) * cap
    spread = ((slot >= first) & (slot < first + cap)).astype(jnp.float32)
    rank_at = jnp.dot(rank, spread, preferred_element_type=jnp.float32)
    named_at = jnp.dot(named, spread, preferred_element_type=jnp.float32)
    place = (lax.broadcasted_iota(jnp.int32, (rows, slots), 1) % cap).astype(jnp.float32)
    return jnp.where((named_at > 0.5) & (rank_at == place), 1.0, 0.0)


def pack_kernel(place_ref, *refs, sources, classes, cap, choose, known):
    x_refs = refs[:sources]
    if known:
        choice_ref = refs[sources]
        piece_refs = refs[sources + 1 :]
        choice = choice_ref[...]
    else:
        *piece_refs, choice_ref = refs[sources:]
        width = x_refs[0].shape[1]
        meta = x_refs[0][:, width - LANES :].astype(jnp.float32)
        choice = choose_slots(meta, place_ref[0], place_ref[1], classes, cap, choose)
        choice_ref[...] = choice
    picks = choice.astype(jnp.bfloat16)
    length = classes * cap // len(piece_refs)
    place = 0
    tile = 16 * LANES
    for x_ref in reversed(x_refs):
        width = x_ref.shape[1]
        for start in range(0, width, tile):
            stop = min(start + tile, width)
            packed = lax.dot_general(
                picks,
                x_ref[:, start:stop],
                (((0,), (0,)), ((), ())),
                preferred_element_type=jnp.float32,
            ).astype(jnp.bfloat16)
            for index, piece_ref in enumerate(piece_refs):
                piece_ref[:, place + start : place + stop] = packed[
                    index * length : (index + 1) * length
                ]
        place += width


def pack(place, chunks, pieces, classes, cap, choose, choice=None):
    rows = chunks[0].shape[0]
    width = sum(chunk.shape[1] for chunk in chunks)
    slots = classes * cap
    known = choice is not None
    outs = [jax.ShapeDtypeStruct((slots // pieces, width), jnp.bfloat16)] * pieces
    if not known:
        outs.append(jax.ShapeDtypeStruct((rows, slots), jnp.float32))
    args = [*chunks, choice] if known else chunks
    packed = pl.pallas_call(
        functools.partial(
            pack_kernel,
            sources=len(chunks),
            classes=classes,
            cap=cap,
            choose=choose,
            known=known,
        ),
        in_specs=[pl.BlockSpec(memory_space=pltpu.SMEM)] + [IN_VMEM] * len(args),
        out_specs=[IN_VMEM] * len(outs),
        out_shape=outs,
        compiler_params=pltpu.CompilerParams(vmem_limit_bytes=VMEM_LIMIT),
        name="pack_rest" if known else "pack",
    )(place, *args)
    return packed if known else (packed[:-1], packed[-1])


def views_kernel(core_ref, mine_ref, theirs_ref, own_ref, other_ref, norm_ref, rest, sems):
    core = core_ref[0]
    _, count, total = mine_ref.shape
    half = total // 2
    images = total // BOX
    before = (core * (images // 2) + images - 1) % images * BOX
    after = (core + 1) * (images // 2) % images * BOX
    copies = []

    def fetch(source_ref, source, target, length):
        source = pl.multiple_of(source, BOX)
        copy = pltpu.make_async_copy(
            source_ref.at[0, :, pl.ds(source, length)], target, sems.at[len(copies)]
        )
        copy.start()
        copies.append(copy)

    for source_ref, out_ref in ((mine_ref, own_ref), (theirs_ref, other_ref)):
        fetch(source_ref, core * half, out_ref.at[:, pl.ds(BOX, half)], half)
        fetch(source_ref, before, out_ref.at[:, pl.ds(0, BOX)], BOX)
        fetch(source_ref, after, out_ref.at[:, pl.ds(BOX + half, BOX)], BOX)
        if source_ref is mine_ref:
            fetch(source_ref, (1 - core) * half, rest, half)
    for copy in copies[:4]:
        copy.wait()
    sums = jnp.zeros((count, LANES), jnp.float32)
    for start in range(0, half, LANES):
        for piece in (own_ref[:, BOX + start : BOX + start + LANES], rest[:, start : start + LANES]):
            piece = piece.astype(jnp.float32)
            sums = sums + piece * piece
    norm_ref[...] = column_to_row(jnp.sum(sums, axis=1, keepdims=True), count)
    for copy in copies[4:]:
        copy.wait()


def make_views(core, mine, theirs):
    _, count, total = mine.shape
    ext = jax.ShapeDtypeStruct((count, total // 2 + 2 * BOX), jnp.bfloat16)
    return pl.pallas_call(
        views_kernel,
        in_specs=[pl.BlockSpec(memory_space=pltpu.SMEM), IN_HBM, IN_HBM],
        out_specs=[IN_VMEM, IN_VMEM, IN_VMEM],
        out_shape=[ext, ext, jax.ShapeDtypeStruct((1, count), jnp.float32)],
        scratch_shapes=[
            pltpu.VMEM((count, total // 2), jnp.bfloat16),
            pltpu.SemaphoreType.DMA((7,)),
        ],
        compiler_params=pltpu.CompilerParams(vmem_limit_bytes=VMEM_LIMIT),
        name="make_views",
    )(core, in_hbm(mine), in_hbm(theirs))


def score_kernel(*refs, pieces, spans, masked, added):
    x_refs = refs[:pieces]
    own_ref, other_ref, norm_ref = refs[pieces : pieces + 3]
    out_ref = refs[-1]
    rows = sum(ref.shape[0] for ref in x_refs)
    count = own_ref.shape[0]
    span = 2 * count
    one = jnp.zeros((rows, LANES), jnp.bfloat16)
    two = jnp.zeros((rows, 2 * LANES), jnp.bfloat16)
    total = None
    for place, start, tile in tiles_of(spans):
        image = joined(x_refs, place, place + tile)
        stack = [
            [one, image, one],
            [image, two],
            [two, image],
            [one, roll_lanes(image, -1), one],
            [one, roll_lanes(image, 1), one],
        ]
        stack = jnp.concatenate([jnp.concatenate(line, axis=1) for line in stack], axis=0)
        stop = start + tile + 2 * LANES
        both = jnp.concatenate([own_ref[:, start:stop], other_ref[:, start:stop]], axis=0)
        part = lax.dot_general(
            stack, both, (((1,), (1,)), ((), ())), preferred_element_type=jnp.float32
        )
        total = part if total is None else total + part
    if masked:
        width = x_refs[0].shape[1]
        keep = joined(x_refs, width - LANES - count, width - LANES).astype(jnp.float32)
        offset = jnp.where(keep > 0.5, 0.0, NEG) - 0.5 * norm_ref[...]
        offset = jnp.concatenate([offset, jnp.zeros_like(offset)], axis=1)
    for index in range(shift_count):
        block = slice(index * span, (index + 1) * span)
        value = total[index * rows : (index + 1) * rows]
        if masked:
            value = value + offset
        if added:
            value = value + refs[pieces + 3][:, block]
        out_ref[:, block] = value


def half_scores(records, own, other, norms, spans, masked, earlier=None):
    rows = sum(piece.shape[0] for piece in records)
    count = own.shape[0]
    args = [*records, own, other, norms]
    if earlier is not None:
        args.append(earlier)
    return pl.pallas_call(
        functools.partial(
            score_kernel,
            pieces=len(records),
            spans=spans,
            masked=masked,
            added=earlier is not None,
        ),
        in_specs=[IN_VMEM] * len(args),
        out_specs=IN_VMEM,
        out_shape=jax.ShapeDtypeStruct((rows, 2 * shift_count * count), jnp.float32),
        compiler_params=pltpu.CompilerParams(vmem_limit_bytes=VMEM_LIMIT),
        name="half_scores",
    )(*args)


def weigh(mine_ref, theirs_ref, tau, count, weight_ref):
    rows = tau.shape[0]
    span = 2 * count
    scores = []
    peak = jnp.full((rows, 1), NEG, jnp.float32)
    for index in range(shift_count):
        mine = mine_ref[:, index * span : (index + 1) * span]
        theirs = theirs_ref[:, index * span : (index + 1) * span]
        swapped = jnp.concatenate([theirs[:, count:], theirs[:, :count]], axis=1)
        full = mine + swapped
        score = jnp.where(full > -1e29, tau * full, NEG)
        scores.append(score)
        peak = jnp.maximum(peak, jnp.max(score, axis=1, keepdims=True))
    total = jnp.zeros((rows, 1), jnp.float32)
    for index, score in enumerate(scores):
        weight = jnp.where(score > -1e28, jnp.exp(score - peak), 0.0).astype(jnp.bfloat16)
        total = total + jnp.sum(weight.astype(jnp.float32), axis=1, keepdims=True)
        weight_ref[index * rows : (index + 1) * rows, :] = weight
    filled = total > 0
    safe = jnp.where(filled, total, 1.0)
    return 1.0 / safe, put_log(jnp.where(filled, peak + jnp.log(safe), NEG), rows)


def write_means(weight_ref, inverse, own_ref, other_ref, out_refs, start, stop):
    length = out_refs[0].shape[0]
    rows = length * len(out_refs)
    weights = weight_ref[...]
    for place, first, tile in tiles_of([(0, start, stop - start)]):
        end = first + tile + 2 * LANES
        both = jnp.concatenate([own_ref[:, first:end], other_ref[:, first:end]], axis=0)
        sums = jnp.dot(weights, both, preferred_element_type=jnp.float32)
        inner = slice(LANES, LANES + tile)
        mean = sums[0:rows, inner] + sums[rows : 2 * rows, 0:tile]
        mean = mean + sums[2 * rows : 3 * rows, 2 * LANES : 2 * LANES + tile]
        mean = mean + roll_lanes(sums[3 * rows : 4 * rows, inner], 1)
        mean = mean + roll_lanes(sums[4 * rows : 5 * rows, inner], -1)
        mean = (mean * inverse).astype(jnp.bfloat16)
        for index, out_ref in enumerate(out_refs):
            out_ref[:, place : place + tile] = mean[index * length : (index + 1) * length]


def mean_kernel(mine_ref, theirs_ref, *refs, chunk, pieces):
    x_refs = refs[:pieces]
    own_ref, other_ref = refs[pieces : pieces + 2]
    out_refs = refs[pieces + 2 : 2 * pieces + 2]
    weight_ref, inverse_ref = refs[2 * pieces + 2 :]
    length, width = x_refs[0].shape
    tau = joined(x_refs, width - LANES, width)[:, 0:1].astype(jnp.float32)
    inverse, logs = weigh(mine_ref, theirs_ref, tau, own_ref.shape[0], weight_ref)
    inverse_ref[...] = jnp.broadcast_to(inverse, inverse_ref.shape)
    start, stop = chunk
    for index, out_ref in enumerate(out_refs):
        out_ref[:, stop - start :] = logs[index * length : (index + 1) * length]
    write_means(weight_ref, inverse, own_ref, other_ref, out_refs, start, stop)


def weighted_means(mine, theirs, records, own, other, chunk):
    length = records[0].shape[0]
    pieces = len(records)
    count = own.shape[0]
    outs = [jax.ShapeDtypeStruct((length, chunk[1] - chunk[0] + LANES), jnp.bfloat16)] * pieces
    outs += [
        jax.ShapeDtypeStruct((shift_count * pieces * length, 2 * count), jnp.bfloat16),
        jax.ShapeDtypeStruct((pieces * length, LANES), jnp.float32),
    ]
    *means, weights, inverse = pl.pallas_call(
        functools.partial(mean_kernel, chunk=chunk, pieces=pieces),
        in_specs=[IN_VMEM] * (pieces + 4),
        out_specs=[IN_VMEM] * len(outs),
        out_shape=outs,
        compiler_params=pltpu.CompilerParams(vmem_limit_bytes=VMEM_LIMIT),
        name="weighted_means",
    )(mine, theirs, *records, own, other)
    return means, weights, inverse


def rest_kernel(weight_ref, inverse_ref, own_ref, other_ref, *out_refs, chunk):
    write_means(weight_ref, inverse_ref[:, 0:1], own_ref, other_ref, out_refs, *chunk)


def rest_of_means(weights, inverse, own, other, chunk, pieces):
    length = inverse.shape[0] // pieces
    return pl.pallas_call(
        functools.partial(rest_kernel, chunk=chunk),
        in_specs=[IN_VMEM] * 4,
        out_specs=[IN_VMEM] * pieces,
        out_shape=[jax.ShapeDtypeStruct((length, chunk[1] - chunk[0]), jnp.bfloat16)] * pieces,
        compiler_params=pltpu.CompilerParams(vmem_limit_bytes=VMEM_LIMIT),
        name="rest_of_means",
    )(weights, inverse, own, other)


def half_mix_kernel(choice_ref, *refs, pieces):
    back_refs = refs[:pieces]
    out_ref, mixer_ref = refs[pieces:]
    rows, slots = choice_ref.shape
    width = out_ref.shape[1] - LANES
    chosen = choice_ref[...] > 0.5
    row = column_to_row(get_log(joined(back_refs, width, width + LANES)), slots)
    value = jnp.where(chosen, row, NEG)
    best = jnp.max(value, axis=1, keepdims=True)
    factor = jnp.where(chosen, jnp.exp(value - best), 0.0)
    total = jnp.sum(factor, axis=1, keepdims=True)
    filled = total > 0
    safe = jnp.where(filled, total, 1.0)
    mixer = jnp.concatenate(split3(factor / safe), axis=0)
    mixer_ref[...] = mixer
    out_ref[:, width:] = put_log(jnp.where(filled, best + jnp.log(safe), NEG), rows)
    write_mix(mixer, back_refs, out_ref, width)


def write_mix(mixer, back_refs, out_ref, width):
    rows = out_ref.shape[0]
    for place, _, tile in tiles_of([(0, 0, width)]):
        images = joined(back_refs, place, place + tile)
        mixed = jnp.dot(mixer, images, preferred_element_type=jnp.float32)
        mixed = mixed[0:rows] + (mixed[rows : 2 * rows] + mixed[2 * rows : 3 * rows])
        out_ref[:, place : place + tile] = mixed.astype(jnp.bfloat16)


def rest_mix_kernel(mixer_ref, *refs):
    *back_refs, out_ref = refs
    write_mix(mixer_ref[...], back_refs, out_ref, out_ref.shape[1])


def half_mix(choice, back):
    rows, slots = choice.shape
    return pl.pallas_call(
        functools.partial(half_mix_kernel, pieces=len(back)),
        in_specs=[IN_VMEM] * (1 + len(back)),
        out_specs=[IN_VMEM] * 2,
        out_shape=[
            jax.ShapeDtypeStruct((rows, back[0].shape[1]), jnp.bfloat16),
            jax.ShapeDtypeStruct((3 * rows, slots), jnp.bfloat16),
        ],
        compiler_params=pltpu.CompilerParams(vmem_limit_bytes=VMEM_LIMIT),
        name="half_mix",
    )(choice, *back)


def rest_of_mix(mixer, back):
    rows = mixer.shape[0] // 3
    return pl.pallas_call(
        rest_mix_kernel,
        in_specs=[IN_VMEM] * (1 + len(back)),
        out_specs=IN_VMEM,
        out_shape=jax.ShapeDtypeStruct((rows, back[0].shape[1]), jnp.bfloat16),
        compiler_params=pltpu.CompilerParams(vmem_limit_bytes=VMEM_LIMIT),
        name="rest_of_mix",
    )(mixer, *back)


def final_kernel(choice_ref, *refs, pieces, chunks):
    back_refs = refs[:pieces]
    part_refs = refs[pieces:-1]
    out_ref = refs[-1]
    rows, slots = choice_ref.shape
    pixels = chunks[-1][1]
    end = chunks[0][1]
    chosen = choice_ref[...] > 0.5
    row = column_to_row(get_log(joined(back_refs, pixels, pixels + LANES)), slots)
    value = jnp.where(chosen, row, NEG)
    part = get_log(part_refs[0][:, end:])
    best = jnp.maximum(jnp.max(value, axis=1, keepdims=True), part)
    factor = jnp.where(chosen, jnp.exp(value - best), 0.0)
    part_factor = jnp.where(part > -1e29, jnp.exp(part - best), 0.0)
    total = jnp.sum(factor, axis=1, keepdims=True) + part_factor
    safe = jnp.where(total > 0, total, 1.0)
    part_factor = part_factor / safe
    mixer = jnp.concatenate(split3(factor / safe), axis=0)
    for (first, last), part_ref in zip(chunks, part_refs):
        for place, start, tile in tiles_of([(0, first, last - first)]):
            images = joined(back_refs, start, start + tile)
            mixed = jnp.dot(mixer, images, preferred_element_type=jnp.float32)
            mixed = mixed[0:rows] + (mixed[rows : 2 * rows] + mixed[2 * rows : 3 * rows])
            mixed = mixed + part_factor * part_ref[:, place : place + tile].astype(jnp.float32)
            out_ref[:, start : start + tile] = mixed.astype(jnp.bfloat16)


def final_mix(choice, back, parts, chunks):
    rows = choice.shape[0]
    args = [choice, *back, *parts]
    return pl.pallas_call(
        functools.partial(final_kernel, pieces=len(back), chunks=chunks),
        in_specs=[IN_VMEM] * len(args),
        out_specs=IN_VMEM,
        out_shape=jax.ShapeDtypeStruct((rows, chunks[-1][1]), jnp.bfloat16),
        compiler_params=pltpu.CompilerParams(vmem_limit_bytes=VMEM_LIMIT),
        name="final_mix",
    )(*args)


def trade(pieces, peers):
    if len(pieces) == peers:
        return [pieces[0]] + [
            lax.ppermute(pieces[flip], "lo", [(i, i ^ flip) for i in range(peers)])
            for flip in range(1, peers)
        ]
    whole = pieces[0]
    parts = whole.reshape(peers, whole.shape[0] // peers, whole.shape[1])
    parts = lax.all_to_all(parts, "lo", split_axis=0, concat_axis=0, tiled=True)
    return [parts.reshape(whole.shape)]


def on_device(particles, tau, candidates, prune, projections):
    halves = lax.axis_size("hi")
    peers = lax.axis_size("lo")
    cores = lax.axis_size("ori")
    core = lax.axis_index("ori")
    part_rows, choose = candidates.shape
    pixels = particles.shape[1] // cores
    count = prune.shape[1]
    cap = 2 * part_rows * choose // (halves * peers)
    lo = lax.axis_index("lo").astype(jnp.int32)
    base = lax.axis_index("hi").astype(jnp.int32) * peers
    pieces = piece_count(peers)
    natural = jnp.stack([base, jnp.zeros_like(lo)])
    place = jnp.stack([base, lo if pieces == peers else jnp.zeros_like(lo)])
    across = [(i, (i + 1) % halves) for i in range(halves)]
    swap = [(i, (i + 1) % cores) for i in range(cores)]

    core_id = core.astype(jnp.int32).reshape(1)
    sent = cut(pixels, SENT_SHARE)
    first, last = sent[0][1], pixels - sent[0][1]
    given = cut(pixels, GIVEN_SHARE)
    payload = make_payload(core_id, particles, tau, candidates, prune, sent)
    far_payload = [lax.ppermute(chunk, "hi", across) for chunk in payload]

    sent_near, choice_near = pack(place, payload, pieces, peers, cap, choose)
    records_near = trade(sent_near, peers)

    other = lax.ppermute(projections, "ori", swap)
    own_views, other_views, norms = make_views(core_id, projections, other)
    far_payload[0], own_views = lax.optimization_barrier((far_payload[0], own_views))
    views = (own_views, other_views)

    sent_far, choice_far = pack(place, far_payload[:1], pieces, peers, cap, choose)
    sent_far, records_near[1:3] = lax.optimization_barrier((sent_far, records_near[1:3]))
    records_far = trade(sent_far, peers)
    choice_far, records_far[1 % len(records_far)] = lax.optimization_barrier(
        (choice_far, records_far[1 % len(records_far)])
    )
    rest_far = pack(place, far_payload[1:], pieces, peers, cap, choose, choice_far)
    rest_far, records_near = lax.optimization_barrier((rest_far, records_near))
    records_rest = trade(rest_far, peers)

    spans = ((last, 0, first), (0, first, last))
    near_mine = half_scores(records_near, *views, norms, spans, True)
    near_mine, records_rest = lax.optimization_barrier((near_mine, records_rest))

    mine = half_scores(records_far, *views, norms, ((0, 0, first),), True)
    mine = half_scores(records_rest, *views, norms, ((0, first, last),), False, mine)
    theirs = lax.ppermute(mine, "ori", swap)
    far_means, weights, inverse = weighted_means(mine, theirs, records_far, *views, given[0])
    near_theirs = lax.ppermute(near_mine, "ori", swap)
    near_theirs, far_means = lax.optimization_barrier((near_theirs, far_means))
    back_far = trade(far_means, peers)
    rest_means = rest_of_means(weights, inverse, *views, given[1], len(far_means))
    back_rest = trade(rest_means, peers)
    near_means, _, _ = weighted_means(near_mine, near_theirs, records_near, *views, (0, pixels))
    near_means, back_far = lax.optimization_barrier((near_means, back_far))
    far_mix, mixer = half_mix(choice_far, back_far)
    part_mix = lax.ppermute(far_mix, "hi", across)
    rest_mix = rest_of_mix(mixer, back_rest)
    rest_part = lax.ppermute(rest_mix, "hi", across)
    back_near = trade(near_means, peers)
    return final_mix(choice_near, back_near, (part_mix, rest_part), given)


def solution(mesh):
    grp, cls, ori = (mesh.shape[name] for name in ("grp", "cls", "ori"))
    inner = Mesh(mesh.devices.reshape(grp, 2, cls // 2, ori), ("grp", "hi", "lo", "ori"))
    rows = ("grp", "hi", "lo")
    placed = (
        P(rows, None),
        P(rows),
        P(rows, None),
        P(rows, "ori"),
        P(("hi", "lo"), "ori", None),
    )
    return jax.shard_map(
        on_device, mesh=inner, in_specs=placed, out_specs=P(rows, "ori"), check_vma=False
    )
```

```python
import functools

import jax
import jax.numpy as jnp
from jax import lax
from jax.experimental import pallas as pl
from jax.experimental.pallas import tpu as pltpu
from jax.sharding import Mesh
from jax.sharding import PartitionSpec as P

BOX = 128
LANES = 128
NEG = -1e30
shift_count = 5
GIVEN_SHARE = 4
SENT_SHARE = 4
VMEM_LIMIT = 24 * 1024 * 1024
IN_HBM = pl.BlockSpec(memory_space=pltpu.HBM)
IN_VMEM = pl.BlockSpec(memory_space=pltpu.VMEM)


def in_hbm(array):
    return pltpu.with_memory_space_constraint(array, pltpu.HBM)


def joined(refs, start, stop):
    if len(refs) == 1:
        return refs[0][:, start:stop]
    return jnp.concatenate([ref[:, start:stop] for ref in refs], axis=0)


def tiles_of(spans):
    tile = 16 * LANES
    for place, start, length in spans:
        for offset in range(0, length, tile):
            yield place + offset, start + offset, min(tile, length - offset)


def cut(pixels, *shares):
    ends = [pixels // 8 * share for share in shares] + [pixels]
    return tuple(zip([0] + ends[:-1], ends))


def piece_count(peers):
    return peers if peers <= 4 else 1


def split3(value):
    high = value.astype(jnp.bfloat16)
    rest = value - high.astype(jnp.float32)
    middle = rest.astype(jnp.bfloat16)
    low = (rest - middle.astype(jnp.float32)).astype(jnp.bfloat16)
    return high, middle, low


def put_log(value, rows):
    high, middle, low = split3(value)
    lane = lax.broadcasted_iota(jnp.int32, (rows, LANES), 1)
    pieces = jnp.where(
        lane == 0,
        high.astype(jnp.float32),
        jnp.where(
            lane == 1,
            middle.astype(jnp.float32),
            jnp.where(lane == 2, low.astype(jnp.float32), 0.0),
        ),
    )
    return pieces.astype(jnp.bfloat16)


def get_log(pieces):
    wide = pieces.astype(jnp.float32)
    return (wide[:, 0:1] + wide[:, 1:2]) + wide[:, 2:3]


def column_to_row(column, count):
    eye = lax.broadcasted_iota(jnp.int32, (count, count), 0) == lax.broadcasted_iota(
        jnp.int32, (count, count), 1
    )
    return jnp.sum(jnp.where(eye, column, 0.0), axis=0, keepdims=True)


def roll_lanes(block, amount):
    pieces = [
        pltpu.roll(block[:, start : start + LANES], amount % LANES, 1)
        for start in range(0, block.shape[1], LANES)
    ]
    return jnp.concatenate(pieces, axis=1)


def payload_kernel(
    core_ref, x_ref, tau_ref, classes_ref, keep_ref, *refs, chunks
):
    out_refs = refs[: len(chunks)]
    tau_scr, classes_scr, keep_scr, sems = refs[len(chunks) :]
    first_ref = out_refs[0]
    rows = first_ref.shape[0]
    count = keep_scr.shape[1]
    pixels = chunks[-1][1]
    copies = [
        pltpu.make_async_copy(tau_ref, tau_scr, sems.at[0]),
        pltpu.make_async_copy(classes_ref, classes_scr, sems.at[1]),
        pltpu.make_async_copy(keep_ref, keep_scr, sems.at[2]),
    ]
    for out_ref, (start, stop) in zip(out_refs, chunks):
        source = pl.multiple_of(core_ref[0] * pixels + start, LANES)
        copies.append(
            pltpu.make_async_copy(
                x_ref.at[:, pl.ds(source, stop - start)],
                out_ref.at[:, pl.ds(0, stop - start)],
                sems.at[len(copies)],
            )
        )
    for copy in copies:
        copy.start()
    for copy in copies[:3]:
        copy.wait()
    end = chunks[0][1]
    keep = keep_scr[...].astype(jnp.float32).astype(jnp.bfloat16)
    first_ref[:, end : end + count] = keep
    eye = lax.broadcasted_iota(jnp.int32, (rows, rows), 0) == lax.broadcasted_iota(
        jnp.int32, (rows, rows), 1
    )
    tau = jnp.sum(
        jnp.where(eye, tau_scr[...].astype(jnp.float32), 0.0), axis=1, keepdims=True
    )
    lane = lax.broadcasted_iota(jnp.int32, (rows, LANES), 1)
    meta = jnp.where(lane == 0, tau, 0.0)
    for j in range(classes_scr.shape[0]):
        named = classes_scr[j : j + 1, :].astype(jnp.float32)
        named = jnp.sum(jnp.where(eye, named, 0.0), axis=1, keepdims=True)
        meta = jnp.where(lane == 1 + j, named, meta)
    first_ref[:, end + count :] = meta.astype(jnp.bfloat16)
    for copy in copies[3:]:
        copy.wait()


def make_payload(core, particles, tau, candidates, prune, chunks):
    rows, choose = candidates.shape
    count = prune.shape[1]
    widths = [stop - start for start, stop in chunks]
    widths[0] += count + LANES
    return pl.pallas_call(
        functools.partial(payload_kernel, chunks=chunks),
        in_specs=[pl.BlockSpec(memory_space=pltpu.SMEM)] + [IN_HBM] * 4,
        out_specs=[IN_VMEM] * len(chunks),
        out_shape=[jax.ShapeDtypeStruct((rows, width), jnp.bfloat16) for width in widths],
        scratch_shapes=[
            pltpu.VMEM((1, rows), jnp.bfloat16),
            pltpu.VMEM((choose, rows), jnp.int32),
            pltpu.VMEM((rows, count), jnp.int32),
            pltpu.SemaphoreType.DMA((3 + len(chunks),)),
        ],
        compiler_params=pltpu.CompilerParams(vmem_limit_bytes=VMEM_LIMIT),
        name="make_payload",
    )(core, *(in_hbm(x) for x in (particles, tau.reshape(1, rows), candidates.T, prune)))


def choose_slots(meta, base, flip, classes, cap, choose):
    rows = meta.shape[0]
    slots = classes * cap
    ids = base + (lax.broadcasted_iota(jnp.int32, (rows, classes), 1) ^ flip)
    ids = ids.astype(jnp.float32)
    named = jnp.zeros((rows, classes), jnp.float32)
    for j in range(choose):
        named = jnp.where(meta[:, 1 + j : 2 + j] == ids, 1.0, named)
    earlier = (
        lax.broadcasted_iota(jnp.int32, (rows, rows), 0)
        > lax.broadcasted_iota(jnp.int32, (rows, rows), 1)
    ).astype(jnp.float32)
    rank = jnp.dot(earlier, named, preferred_element_type=jnp.float32)
    slot = lax.broadcasted_iota(jnp.int32, (classes, slots), 1)
    first = lax.broadcasted_iota(jnp.int32, (classes, slots), 0) * cap
    spread = ((slot >= first) & (slot < first + cap)).astype(jnp.float32)
    rank_at = jnp.dot(rank, spread, preferred_element_type=jnp.float32)
    named_at = jnp.dot(named, spread, preferred_element_type=jnp.float32)
    place = (lax.broadcasted_iota(jnp.int32, (rows, slots), 1) % cap).astype(jnp.float32)
    return jnp.where((named_at > 0.5) & (rank_at == place), 1.0, 0.0)


def pack_kernel(place_ref, *refs, sources, classes, cap, choose, known):
    x_refs = refs[:sources]
    if known:
        choice_ref = refs[sources]
        piece_refs = refs[sources + 1 :]
        choice = choice_ref[...]
    else:
        *piece_refs, choice_ref = refs[sources:]
        width = x_refs[0].shape[1]
        meta = x_refs[0][:, width - LANES :].astype(jnp.float32)
        choice = choose_slots(meta, place_ref[0], place_ref[1], classes, cap, choose)
        choice_ref[...] = choice
    picks = choice.astype(jnp.bfloat16)
    length = classes * cap // len(piece_refs)
    place = 0
    tile = 16 * LANES
    for x_ref in reversed(x_refs):
        width = x_ref.shape[1]
        for start in range(0, width, tile):
            stop = min(start + tile, width)
            packed = lax.dot_general(
                picks,
                x_ref[:, start:stop],
                (((0,), (0,)), ((), ())),
                preferred_element_type=jnp.float32,
            ).astype(jnp.bfloat16)
            for index, piece_ref in enumerate(piece_refs):
                piece_ref[:, place + start : place + stop] = packed[
                    index * length : (index + 1) * length
                ]
        place += width


def pack(place, chunks, pieces, classes, cap, choose, choice=None):
    rows = chunks[0].shape[0]
    width = sum(chunk.shape[1] for chunk in chunks)
    slots = classes * cap
    known = choice is not None
    outs = [jax.ShapeDtypeStruct((slots // pieces, width), jnp.bfloat16)] * pieces
    if not known:
        outs.append(jax.ShapeDtypeStruct((rows, slots), jnp.float32))
    args = [*chunks, choice] if known else chunks
    packed = pl.pallas_call(
        functools.partial(
            pack_kernel,
            sources=len(chunks),
            classes=classes,
            cap=cap,
            choose=choose,
            known=known,
        ),
        in_specs=[pl.BlockSpec(memory_space=pltpu.SMEM)] + [IN_VMEM] * len(args),
        out_specs=[IN_VMEM] * len(outs),
        out_shape=outs,
        compiler_params=pltpu.CompilerParams(vmem_limit_bytes=VMEM_LIMIT),
        name="pack_rest" if known else "pack",
    )(place, *args)
    return packed if known else (packed[:-1], packed[-1])


def views_kernel(core_ref, mine_ref, theirs_ref, own_ref, other_ref, norm_ref, rest, sems):
    core = core_ref[0]
    _, count, total = mine_ref.shape
    half = total // 2
    images = total // BOX
    before = (core * (images // 2) + images - 1) % images * BOX
    after = (core + 1) * (images // 2) % images * BOX
    copies = []

    def fetch(source_ref, source, target, length):
        source = pl.multiple_of(source, BOX)
        copy = pltpu.make_async_copy(
            source_ref.at[0, :, pl.ds(source, length)], target, sems.at[len(copies)]
        )
        copy.start()
        copies.append(copy)

    for source_ref, out_ref in ((mine_ref, own_ref), (theirs_ref, other_ref)):
        fetch(source_ref, core * half, out_ref.at[:, pl.ds(BOX, half)], half)
        fetch(source_ref, before, out_ref.at[:, pl.ds(0, BOX)], BOX)
        fetch(source_ref, after, out_ref.at[:, pl.ds(BOX + half, BOX)], BOX)
        if source_ref is mine_ref:
            fetch(source_ref, (1 - core) * half, rest, half)
    for copy in copies[:4]:
        copy.wait()
    sums = jnp.zeros((count, LANES), jnp.float32)
    for start in range(0, half, LANES):
        for piece in (own_ref[:, BOX + start : BOX + start + LANES], rest[:, start : start + LANES]):
            piece = piece.astype(jnp.float32)
            sums = sums + piece * piece
    norm_ref[...] = column_to_row(jnp.sum(sums, axis=1, keepdims=True), count)
    for copy in copies[4:]:
        copy.wait()


def make_views(core, mine, theirs):
    _, count, total = mine.shape
    ext = jax.ShapeDtypeStruct((count, total // 2 + 2 * BOX), jnp.bfloat16)
    return pl.pallas_call(
        views_kernel,
        in_specs=[pl.BlockSpec(memory_space=pltpu.SMEM), IN_HBM, IN_HBM],
        out_specs=[IN_VMEM, IN_VMEM, IN_VMEM],
        out_shape=[ext, ext, jax.ShapeDtypeStruct((1, count), jnp.float32)],
        scratch_shapes=[
            pltpu.VMEM((count, total // 2), jnp.bfloat16),
            pltpu.SemaphoreType.DMA((7,)),
        ],
        compiler_params=pltpu.CompilerParams(vmem_limit_bytes=VMEM_LIMIT),
        name="make_views",
    )(core, in_hbm(mine), in_hbm(theirs))


def score_kernel(*refs, pieces, spans, masked, added):
    x_refs = refs[:pieces]
    own_ref, other_ref, norm_ref = refs[pieces : pieces + 3]
    out_ref = refs[-1]
    rows = sum(ref.shape[0] for ref in x_refs)
    count = own_ref.shape[0]
    span = 2 * count
    one = jnp.zeros((rows, LANES), jnp.bfloat16)
    two = jnp.zeros((rows, 2 * LANES), jnp.bfloat16)
    total = None
    for place, start, tile in tiles_of(spans):
        image = joined(x_refs, place, place + tile)
        stack = [
            [one, image, one],
            [image, two],
            [two, image],
            [one, roll_lanes(image, -1), one],
            [one, roll_lanes(image, 1), one],
        ]
        stack = jnp.concatenate([jnp.concatenate(line, axis=1) for line in stack], axis=0)
        stop = start + tile + 2 * LANES
        both = jnp.concatenate([own_ref[:, start:stop], other_ref[:, start:stop]], axis=0)
        part = lax.dot_general(
            stack, both, (((1,), (1,)), ((), ())), preferred_element_type=jnp.float32
        )
        total = part if total is None else total + part
    if masked:
        width = x_refs[0].shape[1]
        keep = joined(x_refs, width - LANES - count, width - LANES).astype(jnp.float32)
        offset = jnp.where(keep > 0.5, 0.0, NEG) - 0.5 * norm_ref[...]
        offset = jnp.concatenate([offset, jnp.zeros_like(offset)], axis=1)
    for index in range(shift_count):
        block = slice(index * span, (index + 1) * span)
        value = total[index * rows : (index + 1) * rows]
        if masked:
            value = value + offset
        if added:
            value = value + refs[pieces + 3][:, block]
        out_ref[:, block] = value


def half_scores(records, own, other, norms, spans, masked, earlier=None):
    rows = sum(piece.shape[0] for piece in records)
    count = own.shape[0]
    args = [*records, own, other, norms]
    if earlier is not None:
        args.append(earlier)
    return pl.pallas_call(
        functools.partial(
            score_kernel,
            pieces=len(records),
            spans=spans,
            masked=masked,
            added=earlier is not None,
        ),
        in_specs=[IN_VMEM] * len(args),
        out_specs=IN_VMEM,
        out_shape=jax.ShapeDtypeStruct((rows, 2 * shift_count * count), jnp.float32),
        compiler_params=pltpu.CompilerParams(vmem_limit_bytes=VMEM_LIMIT),
        name="half_scores",
    )(*args)


def weigh(mine_ref, theirs_ref, tau, count, weight_ref):
    rows = tau.shape[0]
    span = 2 * count
    scores = []
    peak = jnp.full((rows, 1), NEG, jnp.float32)
    for index in range(shift_count):
        mine = mine_ref[:, index * span : (index + 1) * span]
        theirs = theirs_ref[:, index * span : (index + 1) * span]
        swapped = jnp.concatenate([theirs[:, count:], theirs[:, :count]], axis=1)
        full = mine + swapped
        score = jnp.where(full > -1e29, tau * full, NEG)
        scores.append(score)
        peak = jnp.maximum(peak, jnp.max(score, axis=1, keepdims=True))
    total = jnp.zeros((rows, 1), jnp.float32)
    for index, score in enumerate(scores):
        weight = jnp.where(score > -1e28, jnp.exp(score - peak), 0.0).astype(jnp.bfloat16)
        total = total + jnp.sum(weight.astype(jnp.float32), axis=1, keepdims=True)
        weight_ref[index * rows : (index + 1) * rows, :] = weight
    filled = total > 0
    safe = jnp.where(filled, total, 1.0)
    return 1.0 / safe, put_log(jnp.where(filled, peak + jnp.log(safe), NEG), rows)


def write_means(weight_ref, inverse, own_ref, other_ref, out_refs, start, stop):
    length = out_refs[0].shape[0]
    rows = length * len(out_refs)
    weights = weight_ref[...]
    for place, first, tile in tiles_of([(0, start, stop - start)]):
        end = first + tile + 2 * LANES
        both = jnp.concatenate([own_ref[:, first:end], other_ref[:, first:end]], axis=0)
        sums = jnp.dot(weights, both, preferred_element_type=jnp.float32)
        inner = slice(LANES, LANES + tile)
        mean = sums[0:rows, inner] + sums[rows : 2 * rows, 0:tile]
        mean = mean + sums[2 * rows : 3 * rows, 2 * LANES : 2 * LANES + tile]
        mean = mean + roll_lanes(sums[3 * rows : 4 * rows, inner], 1)
        mean = mean + roll_lanes(sums[4 * rows : 5 * rows, inner], -1)
        mean = (mean * inverse).astype(jnp.bfloat16)
        for index, out_ref in enumerate(out_refs):
            out_ref[:, place : place + tile] = mean[index * length : (index + 1) * length]


def mean_kernel(mine_ref, theirs_ref, *refs, chunk, pieces):
    x_refs = refs[:pieces]
    own_ref, other_ref = refs[pieces : pieces + 2]
    out_refs = refs[pieces + 2 : 2 * pieces + 2]
    weight_ref, inverse_ref = refs[2 * pieces + 2 :]
    length, width = x_refs[0].shape
    tau = joined(x_refs, width - LANES, width)[:, 0:1].astype(jnp.float32)
    inverse, logs = weigh(mine_ref, theirs_ref, tau, own_ref.shape[0], weight_ref)
    inverse_ref[...] = jnp.broadcast_to(inverse, inverse_ref.shape)
    start, stop = chunk
    for index, out_ref in enumerate(out_refs):
        out_ref[:, stop - start :] = logs[index * length : (index + 1) * length]
    write_means(weight_ref, inverse, own_ref, other_ref, out_refs, start, stop)


def weighted_means(mine, theirs, records, own, other, chunk):
    length = records[0].shape[0]
    pieces = len(records)
    count = own.shape[0]
    outs = [jax.ShapeDtypeStruct((length, chunk[1] - chunk[0] + LANES), jnp.bfloat16)] * pieces
    outs += [
        jax.ShapeDtypeStruct((shift_count * pieces * length, 2 * count), jnp.bfloat16),
        jax.ShapeDtypeStruct((pieces * length, LANES), jnp.float32),
    ]
    *means, weights, inverse = pl.pallas_call(
        functools.partial(mean_kernel, chunk=chunk, pieces=pieces),
        in_specs=[IN_VMEM] * (pieces + 4),
        out_specs=[IN_VMEM] * len(outs),
        out_shape=outs,
        compiler_params=pltpu.CompilerParams(vmem_limit_bytes=VMEM_LIMIT),
        name="weighted_means",
    )(mine, theirs, *records, own, other)
    return means, weights, inverse


def rest_kernel(weight_ref, inverse_ref, own_ref, other_ref, *out_refs, chunk):
    write_means(weight_ref, inverse_ref[:, 0:1], own_ref, other_ref, out_refs, *chunk)


def rest_of_means(weights, inverse, own, other, chunk, pieces):
    length = inverse.shape[0] // pieces
    return pl.pallas_call(
        functools.partial(rest_kernel, chunk=chunk),
        in_specs=[IN_VMEM] * 4,
        out_specs=[IN_VMEM] * pieces,
        out_shape=[jax.ShapeDtypeStruct((length, chunk[1] - chunk[0]), jnp.bfloat16)] * pieces,
        compiler_params=pltpu.CompilerParams(vmem_limit_bytes=VMEM_LIMIT),
        name="rest_of_means",
    )(weights, inverse, own, other)


def half_mix_kernel(choice_ref, *refs, pieces):
    back_refs = refs[:pieces]
    out_ref, mixer_ref = refs[pieces:]
    rows, slots = choice_ref.shape
    width = out_ref.shape[1] - LANES
    chosen = choice_ref[...] > 0.5
    row = column_to_row(get_log(joined(back_refs, width, width + LANES)), slots)
    value = jnp.where(chosen, row, NEG)
    best = jnp.max(value, axis=1, keepdims=True)
    factor = jnp.where(chosen, jnp.exp(value - best), 0.0)
    total = jnp.sum(factor, axis=1, keepdims=True)
    filled = total > 0
    safe = jnp.where(filled, total, 1.0)
    mixer = jnp.concatenate(split3(factor / safe), axis=0)
    mixer_ref[...] = mixer
    out_ref[:, width:] = put_log(jnp.where(filled, best + jnp.log(safe), NEG), rows)
    write_mix(mixer, back_refs, out_ref, width)


def write_mix(mixer, back_refs, out_ref, width):
    rows = out_ref.shape[0]
    for place, _, tile in tiles_of([(0, 0, width)]):
        images = joined(back_refs, place, place + tile)
        mixed = jnp.dot(mixer, images, preferred_element_type=jnp.float32)
        mixed = mixed[0:rows] + (mixed[rows : 2 * rows] + mixed[2 * rows : 3 * rows])
        out_ref[:, place : place + tile] = mixed.astype(jnp.bfloat16)


def rest_mix_kernel(mixer_ref, *refs):
    *back_refs, out_ref = refs
    write_mix(mixer_ref[...], back_refs, out_ref, out_ref.shape[1])


def half_mix(choice, back):
    rows, slots = choice.shape
    return pl.pallas_call(
        functools.partial(half_mix_kernel, pieces=len(back)),
        in_specs=[IN_VMEM] * (1 + len(back)),
        out_specs=[IN_VMEM] * 2,
        out_shape=[
            jax.ShapeDtypeStruct((rows, back[0].shape[1]), jnp.bfloat16),
            jax.ShapeDtypeStruct((3 * rows, slots), jnp.bfloat16),
        ],
        compiler_params=pltpu.CompilerParams(vmem_limit_bytes=VMEM_LIMIT),
        name="half_mix",
    )(choice, *back)


def rest_of_mix(mixer, back):
    rows = mixer.shape[0] // 3
    return pl.pallas_call(
        rest_mix_kernel,
        in_specs=[IN_VMEM] * (1 + len(back)),
        out_specs=IN_VMEM,
        out_shape=jax.ShapeDtypeStruct((rows, back[0].shape[1]), jnp.bfloat16),
        compiler_params=pltpu.CompilerParams(vmem_limit_bytes=VMEM_LIMIT),
        name="rest_of_mix",
    )(mixer, *back)


def final_kernel(choice_ref, *refs, pieces, chunks):
    back_refs = refs[:pieces]
    part_refs = refs[pieces:-1]
    out_ref = refs[-1]
    rows, slots = choice_ref.shape
    pixels = chunks[-1][1]
    end = chunks[0][1]
    chosen = choice_ref[...] > 0.5
    row = column_to_row(get_log(joined(back_refs, pixels, pixels + LANES)), slots)
    value = jnp.where(chosen, row, NEG)
    part = get_log(part_refs[0][:, end:])
    best = jnp.maximum(jnp.max(value, axis=1, keepdims=True), part)
    factor = jnp.where(chosen, jnp.exp(value - best), 0.0)
    part_factor = jnp.where(part > -1e29, jnp.exp(part - best), 0.0)
    total = jnp.sum(factor, axis=1, keepdims=True) + part_factor
    safe = jnp.where(total > 0, total, 1.0)
    part_factor = part_factor / safe
    mixer = jnp.concatenate(split3(factor / safe), axis=0)
    for (first, last), part_ref in zip(chunks, part_refs):
        for place, start, tile in tiles_of([(0, first, last - first)]):
            images = joined(back_refs, start, start + tile)
            mixed = jnp.dot(mixer, images, preferred_element_type=jnp.float32)
            mixed = mixed[0:rows] + (mixed[rows : 2 * rows] + mixed[2 * rows : 3 * rows])
            mixed = mixed + part_factor * part_ref[:, place : place + tile].astype(jnp.float32)
            out_ref[:, start : start + tile] = mixed.astype(jnp.bfloat16)


def final_mix(choice, back, parts, chunks):
    rows = choice.shape[0]
    args = [choice, *back, *parts]
    return pl.pallas_call(
        functools.partial(final_kernel, pieces=len(back), chunks=chunks),
        in_specs=[IN_VMEM] * len(args),
        out_specs=IN_VMEM,
        out_shape=jax.ShapeDtypeStruct((rows, chunks[-1][1]), jnp.bfloat16),
        compiler_params=pltpu.CompilerParams(vmem_limit_bytes=VMEM_LIMIT),
        name="final_mix",
    )(*args)


def trade(pieces, peers):
    if len(pieces) == peers:
        return [pieces[0]] + [
            lax.ppermute(pieces[flip], "lo", [(i, i ^ flip) for i in range(peers)])
            for flip in range(1, peers)
        ]
    whole = pieces[0]
    parts = whole.reshape(peers, whole.shape[0] // peers, whole.shape[1])
    parts = lax.all_to_all(parts, "lo", split_axis=0, concat_axis=0, tiled=True)
    return [parts.reshape(whole.shape)]


def hold_back(early, late, part):
    held, late = lax.optimization_barrier((early[part], late))
    early = list(early)
    early[part] = held
    return early, late


def on_device(particles, tau, candidates, prune, projections):
    halves = lax.axis_size("hi")
    peers = lax.axis_size("lo")
    cores = lax.axis_size("ori")
    core = lax.axis_index("ori")
    part_rows, choose = candidates.shape
    pixels = particles.shape[1] // cores
    count = prune.shape[1]
    cap = 2 * part_rows * choose // (halves * peers)
    lo = lax.axis_index("lo").astype(jnp.int32)
    base = lax.axis_index("hi").astype(jnp.int32) * peers
    pieces = piece_count(peers)
    natural = jnp.stack([base, jnp.zeros_like(lo)])
    place = jnp.stack([base, lo if pieces == peers else jnp.zeros_like(lo)])
    across = [(i, (i + 1) % halves) for i in range(halves)]
    swap = [(i, (i + 1) % cores) for i in range(cores)]

    core_id = core.astype(jnp.int32).reshape(1)
    sent = cut(pixels, SENT_SHARE)
    first, last = sent[0][1], pixels - sent[0][1]
    given = cut(pixels, GIVEN_SHARE)
    payload = make_payload(core_id, particles, tau, candidates, prune, sent)
    far_payload = [lax.ppermute(chunk, "hi", across) for chunk in payload]

    sent_near, choice_near = pack(place, payload, pieces, peers, cap, choose)
    records_near = trade(sent_near, peers)

    other = lax.ppermute(projections, "ori", swap)
    own_views, other_views, norms = make_views(core_id, projections, other)
    far_payload[0], own_views = lax.optimization_barrier((far_payload[0], own_views))
    views = (own_views, other_views)

    sent_far, choice_far = pack(place, far_payload[:1], pieces, peers, cap, choose)
    records_near, sent_far = hold_back(records_near, sent_far, slice(1, 2))
    records_far = trade(sent_far, peers)
    choice_far, records_far[1 % len(records_far)] = lax.optimization_barrier(
        (choice_far, records_far[1 % len(records_far)])
    )
    rest_far = pack(place, far_payload[1:], pieces, peers, cap, choose, choice_far)
    rest_far, records_near = lax.optimization_barrier((rest_far, records_near))
    records_rest = trade(rest_far, peers)

    spans = ((last, 0, first), (0, first, last))
    near_mine = half_scores(records_near, *views, norms, spans, True)
    near_mine, records_rest = lax.optimization_barrier((near_mine, records_rest))

    mine = half_scores(records_far, *views, norms, ((0, 0, first),), True)
    mine = half_scores(records_rest, *views, norms, ((0, first, last),), False, mine)
    theirs = lax.ppermute(mine, "ori", swap)
    far_means, weights, inverse = weighted_means(mine, theirs, records_far, *views, given[0])
    near_theirs = lax.ppermute(near_mine, "ori", swap)
    near_theirs, far_means = lax.optimization_barrier((near_theirs, far_means))
    back_far = trade(far_means, peers)
    rest_means = rest_of_means(weights, inverse, *views, given[1], len(far_means))
    back_rest = trade(rest_means, peers)
    near_means, _, _ = weighted_means(near_mine, near_theirs, records_near, *views, (0, pixels))
    near_means, back_far = lax.optimization_barrier((near_means, back_far))
    far_mix, mixer = half_mix(choice_far, back_far)
    part_mix = lax.ppermute(far_mix, "hi", across)
    rest_mix = rest_of_mix(mixer, back_rest)
    rest_part = lax.ppermute(rest_mix, "hi", across)
    back_near = trade(near_means, peers)
    return final_mix(choice_near, back_near, (part_mix, rest_part), given)


def solution(mesh):
    grp, cls, ori = (mesh.shape[name] for name in ("grp", "cls", "ori"))
    inner = Mesh(mesh.devices.reshape(grp, 2, cls // 2, ori), ("grp", "hi", "lo", "ori"))
    rows = ("grp", "hi", "lo")
    placed = (
        P(rows, None),
        P(rows),
        P(rows, None),
        P(rows, "ori"),
        P(("hi", "lo"), "ori", None),
    )
    return jax.shard_map(
        on_device, mesh=inner, in_specs=placed, out_specs=P(rows, "ori"), check_vma=False
    )
```

```python
import functools

import jax
import jax.numpy as jnp
from jax import lax
from jax.experimental import pallas as pl
from jax.experimental.pallas import tpu as pltpu
from jax.sharding import Mesh
from jax.sharding import PartitionSpec as P

BOX = 128
LANES = 128
NEG = -1e30
shift_count = 5
GIVEN_SHARE = 4
SENT_SHARE = 5
VMEM_LIMIT = 24 * 1024 * 1024
IN_HBM = pl.BlockSpec(memory_space=pltpu.HBM)
IN_VMEM = pl.BlockSpec(memory_space=pltpu.VMEM)


def in_hbm(array):
    return pltpu.with_memory_space_constraint(array, pltpu.HBM)


def joined(refs, start, stop):
    if len(refs) == 1:
        return refs[0][:, start:stop]
    return jnp.concatenate([ref[:, start:stop] for ref in refs], axis=0)


def tiles_of(spans):
    tile = 32 * LANES
    for place, start, length in spans:
        for offset in range(0, length, tile):
            yield place + offset, start + offset, min(tile, length - offset)


def cut(pixels, *shares):
    ends = [pixels // 8 * share for share in shares] + [pixels]
    return tuple(zip([0] + ends[:-1], ends))


def piece_count(peers):
    return peers if peers <= 4 else 1


def split3(value):
    high = value.astype(jnp.bfloat16)
    rest = value - high.astype(jnp.float32)
    middle = rest.astype(jnp.bfloat16)
    low = (rest - middle.astype(jnp.float32)).astype(jnp.bfloat16)
    return high, middle, low


def put_log(value, rows):
    high, middle, low = split3(value)
    lane = lax.broadcasted_iota(jnp.int32, (rows, LANES), 1)
    pieces = jnp.where(
        lane == 0,
        high.astype(jnp.float32),
        jnp.where(
            lane == 1,
            middle.astype(jnp.float32),
            jnp.where(lane == 2, low.astype(jnp.float32), 0.0),
        ),
    )
    return pieces.astype(jnp.bfloat16)


def get_log(pieces):
    wide = pieces.astype(jnp.float32)
    return (wide[:, 0:1] + wide[:, 1:2]) + wide[:, 2:3]


def column_to_row(column, count):
    eye = lax.broadcasted_iota(jnp.int32, (count, count), 0) == lax.broadcasted_iota(
        jnp.int32, (count, count), 1
    )
    return jnp.sum(jnp.where(eye, column, 0.0), axis=0, keepdims=True)


def roll_lanes(block, amount):
    pieces = [
        pltpu.roll(block[:, start : start + LANES], amount % LANES, 1)
        for start in range(0, block.shape[1], LANES)
    ]
    return jnp.concatenate(pieces, axis=1)


def payload_kernel(
    core_ref, x_ref, tau_ref, classes_ref, keep_ref, *refs, chunks
):
    out_refs = refs[: len(chunks)]
    tau_scr, classes_scr, keep_scr, sems = refs[len(chunks) :]
    first_ref = out_refs[0]
    rows = first_ref.shape[0]
    count = keep_scr.shape[1]
    pixels = chunks[-1][1]
    copies = [
        pltpu.make_async_copy(tau_ref, tau_scr, sems.at[0]),
        pltpu.make_async_copy(classes_ref, classes_scr, sems.at[1]),
        pltpu.make_async_copy(keep_ref, keep_scr, sems.at[2]),
    ]
    for out_ref, (start, stop) in zip(out_refs, chunks):
        source = pl.multiple_of(core_ref[0] * pixels + start, LANES)
        copies.append(
            pltpu.make_async_copy(
                x_ref.at[:, pl.ds(source, stop - start)],
                out_ref.at[:, pl.ds(0, stop - start)],
                sems.at[len(copies)],
            )
        )
    for copy in copies:
        copy.start()
    for copy in copies[:3]:
        copy.wait()
    end = chunks[0][1]
    keep = keep_scr[...].astype(jnp.float32).astype(jnp.bfloat16)
    first_ref[:, end : end + count] = keep
    eye = lax.broadcasted_iota(jnp.int32, (rows, rows), 0) == lax.broadcasted_iota(
        jnp.int32, (rows, rows), 1
    )
    tau = jnp.sum(
        jnp.where(eye, tau_scr[...].astype(jnp.float32), 0.0), axis=1, keepdims=True
    )
    lane = lax.broadcasted_iota(jnp.int32, (rows, LANES), 1)
    meta = jnp.where(lane == 0, tau, 0.0)
    for j in range(classes_scr.shape[0]):
        named = classes_scr[j : j + 1, :].astype(jnp.float32)
        named = jnp.sum(jnp.where(eye, named, 0.0), axis=1, keepdims=True)
        meta = jnp.where(lane == 1 + j, named, meta)
    first_ref[:, end + count :] = meta.astype(jnp.bfloat16)
    for copy in copies[3:]:
        copy.wait()


def make_payload(core, particles, tau, candidates, prune, chunks):
    rows, choose = candidates.shape
    count = prune.shape[1]
    widths = [stop - start for start, stop in chunks]
    widths[0] += count + LANES
    return pl.pallas_call(
        functools.partial(payload_kernel, chunks=chunks),
        in_specs=[pl.BlockSpec(memory_space=pltpu.SMEM)] + [IN_HBM] * 4,
        out_specs=[IN_VMEM] * len(chunks),
        out_shape=[jax.ShapeDtypeStruct((rows, width), jnp.bfloat16) for width in widths],
        scratch_shapes=[
            pltpu.VMEM((1, rows), jnp.bfloat16),
            pltpu.VMEM((choose, rows), jnp.int32),
            pltpu.VMEM((rows, count), jnp.int32),
            pltpu.SemaphoreType.DMA((3 + len(chunks),)),
        ],
        compiler_params=pltpu.CompilerParams(vmem_limit_bytes=VMEM_LIMIT),
        name="make_payload",
    )(core, *(in_hbm(x) for x in (particles, tau.reshape(1, rows), candidates.T, prune)))


def choose_slots(meta, base, flip, classes, cap, choose):
    rows = meta.shape[0]
    slots = classes * cap
    ids = base + (lax.broadcasted_iota(jnp.int32, (rows, classes), 1) ^ flip)
    ids = ids.astype(jnp.float32)
    named = jnp.zeros((rows, classes), jnp.float32)
    for j in range(choose):
        named = jnp.where(meta[:, 1 + j : 2 + j] == ids, 1.0, named)
    earlier = (
        lax.broadcasted_iota(jnp.int32, (rows, rows), 0)
        > lax.broadcasted_iota(jnp.int32, (rows, rows), 1)
    ).astype(jnp.float32)
    rank = jnp.dot(earlier, named, preferred_element_type=jnp.float32)
    slot = lax.broadcasted_iota(jnp.int32, (classes, slots), 1)
    first = lax.broadcasted_iota(jnp.int32, (classes, slots), 0) * cap
    spread = ((slot >= first) & (slot < first + cap)).astype(jnp.float32)
    rank_at = jnp.dot(rank, spread, preferred_element_type=jnp.float32)
    named_at = jnp.dot(named, spread, preferred_element_type=jnp.float32)
    place = (lax.broadcasted_iota(jnp.int32, (rows, slots), 1) % cap).astype(jnp.float32)
    return jnp.where((named_at > 0.5) & (rank_at == place), 1.0, 0.0)


def pack_kernel(place_ref, *refs, sources, classes, cap, choose, known):
    x_refs = refs[:sources]
    if known:
        choice_ref = refs[sources]
        piece_refs = refs[sources + 1 :]
        choice = choice_ref[...]
    else:
        *piece_refs, choice_ref = refs[sources:]
        width = x_refs[0].shape[1]
        meta = x_refs[0][:, width - LANES :].astype(jnp.float32)
        choice = choose_slots(meta, place_ref[0], place_ref[1], classes, cap, choose)
        choice_ref[...] = choice
    picks = choice.astype(jnp.bfloat16)
    length = classes * cap // len(piece_refs)
    place = 0
    tile = 16 * LANES
    for x_ref in reversed(x_refs):
        width = x_ref.shape[1]
        for start in range(0, width, tile):
            stop = min(start + tile, width)
            packed = lax.dot_general(
                picks,
                x_ref[:, start:stop],
                (((0,), (0,)), ((), ())),
                preferred_element_type=jnp.float32,
            ).astype(jnp.bfloat16)
            for index, piece_ref in enumerate(piece_refs):
                piece_ref[:, place + start : place + stop] = packed[
                    index * length : (index + 1) * length
                ]
        place += width


def pack(place, chunks, pieces, classes, cap, choose, choice=None):
    rows = chunks[0].shape[0]
    width = sum(chunk.shape[1] for chunk in chunks)
    slots = classes * cap
    known = choice is not None
    outs = [jax.ShapeDtypeStruct((slots // pieces, width), jnp.bfloat16)] * pieces
    if not known:
        outs.append(jax.ShapeDtypeStruct((rows, slots), jnp.float32))
    args = [*chunks, choice] if known else chunks
    packed = pl.pallas_call(
        functools.partial(
            pack_kernel,
            sources=len(chunks),
            classes=classes,
            cap=cap,
            choose=choose,
            known=known,
        ),
        in_specs=[pl.BlockSpec(memory_space=pltpu.SMEM)] + [IN_VMEM] * len(args),
        out_specs=[IN_VMEM] * len(outs),
        out_shape=outs,
        compiler_params=pltpu.CompilerParams(vmem_limit_bytes=VMEM_LIMIT),
        name="pack_rest" if known else "pack",
    )(place, *args)
    return packed if known else (packed[:-1], packed[-1])


def views_kernel(core_ref, mine_ref, theirs_ref, own_ref, other_ref, norm_ref, rest, sems):
    core = core_ref[0]
    _, count, total = mine_ref.shape
    half = total // 2
    images = total // BOX
    before = (core * (images // 2) + images - 1) % images * BOX
    after = (core + 1) * (images // 2) % images * BOX
    copies = []

    def fetch(source_ref, source, target, length):
        source = pl.multiple_of(source, BOX)
        copy = pltpu.make_async_copy(
            source_ref.at[0, :, pl.ds(source, length)], target, sems.at[len(copies)]
        )
        copy.start()
        copies.append(copy)

    for source_ref, out_ref in ((mine_ref, own_ref), (theirs_ref, other_ref)):
        fetch(source_ref, core * half, out_ref.at[:, pl.ds(BOX, half)], half)
        fetch(source_ref, before, out_ref.at[:, pl.ds(0, BOX)], BOX)
        fetch(source_ref, after, out_ref.at[:, pl.ds(BOX + half, BOX)], BOX)
        if source_ref is mine_ref:
            fetch(source_ref, (1 - core) * half, rest, half)
    for copy in copies[:4]:
        copy.wait()
    sums = jnp.zeros((count, LANES), jnp.float32)
    for start in range(0, half, LANES):
        for piece in (own_ref[:, BOX + start : BOX + start + LANES], rest[:, start : start + LANES]):
            piece = piece.astype(jnp.float32)
            sums = sums + piece * piece
    norm_ref[...] = column_to_row(jnp.sum(sums, axis=1, keepdims=True), count)
    for copy in copies[4:]:
        copy.wait()


def make_views(core, mine, theirs):
    _, count, total = mine.shape
    ext = jax.ShapeDtypeStruct((count, total // 2 + 2 * BOX), jnp.bfloat16)
    return pl.pallas_call(
        views_kernel,
        in_specs=[pl.BlockSpec(memory_space=pltpu.SMEM), IN_HBM, IN_HBM],
        out_specs=[IN_VMEM, IN_VMEM, IN_VMEM],
        out_shape=[ext, ext, jax.ShapeDtypeStruct((1, count), jnp.float32)],
        scratch_shapes=[
            pltpu.VMEM((count, total // 2), jnp.bfloat16),
            pltpu.SemaphoreType.DMA((7,)),
        ],
        compiler_params=pltpu.CompilerParams(vmem_limit_bytes=VMEM_LIMIT),
        name="make_views",
    )(core, in_hbm(mine), in_hbm(theirs))


def score_kernel(*refs, pieces, spans, masked, added):
    x_refs = refs[:pieces]
    own_ref, other_ref, norm_ref = refs[pieces : pieces + 3]
    out_ref = refs[-1]
    rows = sum(ref.shape[0] for ref in x_refs)
    count = own_ref.shape[0]
    span = 2 * count
    one = jnp.zeros((rows, LANES), jnp.bfloat16)
    two = jnp.zeros((rows, 2 * LANES), jnp.bfloat16)
    total = None
    for place, start, tile in tiles_of(spans):
        image = joined(x_refs, place, place + tile)
        stack = [
            [one, image, one],
            [image, two],
            [two, image],
            [one, roll_lanes(image, -1), one],
            [one, roll_lanes(image, 1), one],
        ]
        stack = jnp.concatenate([jnp.concatenate(line, axis=1) for line in stack], axis=0)
        stop = start + tile + 2 * LANES
        both = jnp.concatenate([own_ref[:, start:stop], other_ref[:, start:stop]], axis=0)
        part = lax.dot_general(
            stack, both, (((1,), (1,)), ((), ())), preferred_element_type=jnp.float32
        )
        total = part if total is None else total + part
    if masked:
        width = x_refs[0].shape[1]
        keep = joined(x_refs, width - LANES - count, width - LANES).astype(jnp.float32)
        offset = jnp.where(keep > 0.5, 0.0, NEG) - 0.5 * norm_ref[...]
        offset = jnp.concatenate([offset, jnp.zeros_like(offset)], axis=1)
    for index in range(shift_count):
        block = slice(index * span, (index + 1) * span)
        value = total[index * rows : (index + 1) * rows]
        if masked:
            value = value + offset
        if added:
            value = value + refs[pieces + 3][:, block]
        out_ref[:, block] = value


def half_scores(records, own, other, norms, spans, masked, earlier=None):
    rows = sum(piece.shape[0] for piece in records)
    count = own.shape[0]
    args = [*records, own, other, norms]
    if earlier is not None:
        args.append(earlier)
    return pl.pallas_call(
        functools.partial(
            score_kernel,
            pieces=len(records),
            spans=spans,
            masked=masked,
            added=earlier is not None,
        ),
        in_specs=[IN_VMEM] * len(args),
        out_specs=IN_VMEM,
        out_shape=jax.ShapeDtypeStruct((rows, 2 * shift_count * count), jnp.float32),
        compiler_params=pltpu.CompilerParams(vmem_limit_bytes=VMEM_LIMIT),
        name="half_scores",
    )(*args)


def weigh(mine_ref, theirs_ref, tau, count, weight_ref):
    rows = tau.shape[0]
    span = 2 * count
    scores = []
    peak = jnp.full((rows, 1), NEG, jnp.float32)
    for index in range(shift_count):
        mine = mine_ref[:, index * span : (index + 1) * span]
        theirs = theirs_ref[:, index * span : (index + 1) * span]
        swapped = jnp.concatenate([theirs[:, count:], theirs[:, :count]], axis=1)
        full = mine + swapped
        score = jnp.where(full > -1e29, tau * full, NEG)
        scores.append(score)
        peak = jnp.maximum(peak, jnp.max(score, axis=1, keepdims=True))
    total = jnp.zeros((rows, 1), jnp.float32)
    for index, score in enumerate(scores):
        weight = jnp.where(score > -1e28, jnp.exp(score - peak), 0.0).astype(jnp.bfloat16)
        total = total + jnp.sum(weight.astype(jnp.float32), axis=1, keepdims=True)
        weight_ref[index * rows : (index + 1) * rows, :] = weight
    filled = total > 0
    safe = jnp.where(filled, total, 1.0)
    return 1.0 / safe, put_log(jnp.where(filled, peak + jnp.log(safe), NEG), rows)


def write_means(weight_ref, inverse, own_ref, other_ref, out_refs, start, stop):
    length = out_refs[0].shape[0]
    rows = length * len(out_refs)
    weights = weight_ref[...]
    for place, first, tile in tiles_of([(0, start, stop - start)]):
        end = first + tile + 2 * LANES
        both = jnp.concatenate([own_ref[:, first:end], other_ref[:, first:end]], axis=0)
        sums = jnp.dot(weights, both, preferred_element_type=jnp.float32)
        inner = slice(LANES, LANES + tile)
        mean = sums[0:rows, inner] + sums[rows : 2 * rows, 0:tile]
        mean = mean + sums[2 * rows : 3 * rows, 2 * LANES : 2 * LANES + tile]
        mean = mean + roll_lanes(sums[3 * rows : 4 * rows, inner], 1)
        mean = mean + roll_lanes(sums[4 * rows : 5 * rows, inner], -1)
        mean = (mean * inverse).astype(jnp.bfloat16)
        for index, out_ref in enumerate(out_refs):
            out_ref[:, place : place + tile] = mean[index * length : (index + 1) * length]


def mean_kernel(mine_ref, theirs_ref, *refs, chunk, pieces):
    x_refs = refs[:pieces]
    own_ref, other_ref = refs[pieces : pieces + 2]
    out_refs = refs[pieces + 2 : 2 * pieces + 2]
    weight_ref, inverse_ref = refs[2 * pieces + 2 :]
    length, width = x_refs[0].shape
    tau = joined(x_refs, width - LANES, width)[:, 0:1].astype(jnp.float32)
    inverse, logs = weigh(mine_ref, theirs_ref, tau, own_ref.shape[0], weight_ref)
    inverse_ref[...] = jnp.broadcast_to(inverse, inverse_ref.shape)
    start, stop = chunk
    for index, out_ref in enumerate(out_refs):
        out_ref[:, stop - start :] = logs[index * length : (index + 1) * length]
    write_means(weight_ref, inverse, own_ref, other_ref, out_refs, start, stop)


def weighted_means(mine, theirs, records, own, other, chunk):
    length = records[0].shape[0]
    pieces = len(records)
    count = own.shape[0]
    outs = [jax.ShapeDtypeStruct((length, chunk[1] - chunk[0] + LANES), jnp.bfloat16)] * pieces
    outs += [
        jax.ShapeDtypeStruct((shift_count * pieces * length, 2 * count), jnp.bfloat16),
        jax.ShapeDtypeStruct((pieces * length, LANES), jnp.float32),
    ]
    *means, weights, inverse = pl.pallas_call(
        functools.partial(mean_kernel, chunk=chunk, pieces=pieces),
        in_specs=[IN_VMEM] * (pieces + 4),
        out_specs=[IN_VMEM] * len(outs),
        out_shape=outs,
        compiler_params=pltpu.CompilerParams(vmem_limit_bytes=VMEM_LIMIT),
        name="weighted_means",
    )(mine, theirs, *records, own, other)
    return means, weights, inverse


def rest_kernel(weight_ref, inverse_ref, own_ref, other_ref, *out_refs, chunk):
    write_means(weight_ref, inverse_ref[:, 0:1], own_ref, other_ref, out_refs, *chunk)


def rest_of_means(weights, inverse, own, other, chunk, pieces):
    length = inverse.shape[0] // pieces
    return pl.pallas_call(
        functools.partial(rest_kernel, chunk=chunk),
        in_specs=[IN_VMEM] * 4,
        out_specs=[IN_VMEM] * pieces,
        out_shape=[jax.ShapeDtypeStruct((length, chunk[1] - chunk[0]), jnp.bfloat16)] * pieces,
        compiler_params=pltpu.CompilerParams(vmem_limit_bytes=VMEM_LIMIT),
        name="rest_of_means",
    )(weights, inverse, own, other)


def half_mix_kernel(choice_ref, *refs, pieces):
    back_refs = refs[:pieces]
    out_ref, mixer_ref = refs[pieces:]
    rows, slots = choice_ref.shape
    width = out_ref.shape[1] - LANES
    chosen = choice_ref[...] > 0.5
    row = column_to_row(get_log(joined(back_refs, width, width + LANES)), slots)
    value = jnp.where(chosen, row, NEG)
    best = jnp.max(value, axis=1, keepdims=True)
    factor = jnp.where(chosen, jnp.exp(value - best), 0.0)
    total = jnp.sum(factor, axis=1, keepdims=True)
    filled = total > 0
    safe = jnp.where(filled, total, 1.0)
    mixer = jnp.concatenate(split3(factor / safe), axis=0)
    mixer_ref[...] = mixer
    out_ref[:, width:] = put_log(jnp.where(filled, best + jnp.log(safe), NEG), rows)
    write_mix(mixer, back_refs, out_ref, width)


def write_mix(mixer, back_refs, out_ref, width):
    rows = out_ref.shape[0]
    for place, _, tile in tiles_of([(0, 0, width)]):
        images = joined(back_refs, place, place + tile)
        mixed = jnp.dot(mixer, images, preferred_element_type=jnp.float32)
        mixed = mixed[0:rows] + (mixed[rows : 2 * rows] + mixed[2 * rows : 3 * rows])
        out_ref[:, place : place + tile] = mixed.astype(jnp.bfloat16)


def rest_mix_kernel(mixer_ref, *refs):
    *back_refs, out_ref = refs
    write_mix(mixer_ref[...], back_refs, out_ref, out_ref.shape[1])


def half_mix(choice, back):
    rows, slots = choice.shape
    return pl.pallas_call(
        functools.partial(half_mix_kernel, pieces=len(back)),
        in_specs=[IN_VMEM] * (1 + len(back)),
        out_specs=[IN_VMEM] * 2,
        out_shape=[
            jax.ShapeDtypeStruct((rows, back[0].shape[1]), jnp.bfloat16),
            jax.ShapeDtypeStruct((3 * rows, slots), jnp.bfloat16),
        ],
        compiler_params=pltpu.CompilerParams(vmem_limit_bytes=VMEM_LIMIT),
        name="half_mix",
    )(choice, *back)


def rest_of_mix(mixer, back):
    rows = mixer.shape[0] // 3
    return pl.pallas_call(
        rest_mix_kernel,
        in_specs=[IN_VMEM] * (1 + len(back)),
        out_specs=IN_VMEM,
        out_shape=jax.ShapeDtypeStruct((rows, back[0].shape[1]), jnp.bfloat16),
        compiler_params=pltpu.CompilerParams(vmem_limit_bytes=VMEM_LIMIT),
        name="rest_of_mix",
    )(mixer, *back)


def final_kernel(choice_ref, *refs, pieces, chunks):
    back_refs = refs[:pieces]
    *part_refs, out_ref, mixed_ref, sems = refs[pieces:]
    copies = []
    rows, slots = choice_ref.shape
    pixels = chunks[-1][1]
    end = chunks[0][1]
    chosen = choice_ref[...] > 0.5
    row = column_to_row(get_log(joined(back_refs, pixels, pixels + LANES)), slots)
    value = jnp.where(chosen, row, NEG)
    part = get_log(part_refs[0][:, end:])
    best = jnp.maximum(jnp.max(value, axis=1, keepdims=True), part)
    factor = jnp.where(chosen, jnp.exp(value - best), 0.0)
    part_factor = jnp.where(part > -1e29, jnp.exp(part - best), 0.0)
    total = jnp.sum(factor, axis=1, keepdims=True) + part_factor
    safe = jnp.where(total > 0, total, 1.0)
    part_factor = part_factor / safe
    mixer = jnp.concatenate(split3(factor / safe), axis=0)
    for (first, last), part_ref in zip(chunks, part_refs):
        for place, start, tile in tiles_of([(0, first, last - first)]):
            images = joined(back_refs, start, start + tile)
            mixed = jnp.dot(mixer, images, preferred_element_type=jnp.float32)
            mixed = mixed[0:rows] + (mixed[rows : 2 * rows] + mixed[2 * rows : 3 * rows])
            mixed = mixed + part_factor * part_ref[:, place : place + tile].astype(jnp.float32)
            span = pl.ds(start, tile)
            mixed_ref[:, span] = mixed.astype(jnp.bfloat16)
            copy = pltpu.make_async_copy(
                mixed_ref.at[:, span], out_ref.at[:, span], sems.at[len(copies)]
            )
            copy.start()
            copies.append(copy)
    for copy in copies:
        copy.wait()


def final_mix(choice, back, parts, chunks):
    rows = choice.shape[0]
    args = [choice, *back, *parts]
    count = len(list(tiles_of([(0, first, last - first) for first, last in chunks])))
    return pl.pallas_call(
        functools.partial(final_kernel, pieces=len(back), chunks=chunks),
        in_specs=[IN_VMEM] * len(args),
        out_specs=IN_HBM,
        out_shape=jax.ShapeDtypeStruct((rows, chunks[-1][1]), jnp.bfloat16),
        scratch_shapes=[
            pltpu.VMEM((rows, chunks[-1][1]), jnp.bfloat16),
            pltpu.SemaphoreType.DMA((count,)),
        ],
        compiler_params=pltpu.CompilerParams(vmem_limit_bytes=VMEM_LIMIT),
        name="final_mix",
    )(*args)


def trade(pieces, peers):
    if len(pieces) == peers:
        return [pieces[0]] + [
            lax.ppermute(pieces[flip], "lo", [(i, i ^ flip) for i in range(peers)])
            for flip in range(1, peers)
        ]
    whole = pieces[0]
    parts = whole.reshape(peers, whole.shape[0] // peers, whole.shape[1])
    parts = lax.all_to_all(parts, "lo", split_axis=0, concat_axis=0, tiled=True)
    return [parts.reshape(whole.shape)]


def hold_back(early, late, part):
    held, late = lax.optimization_barrier((early[part], late))
    early = list(early)
    early[part] = held
    return early, late


def on_device(particles, tau, candidates, prune, projections):
    halves = lax.axis_size("hi")
    peers = lax.axis_size("lo")
    cores = lax.axis_size("ori")
    core = lax.axis_index("ori")
    part_rows, choose = candidates.shape
    pixels = particles.shape[1] // cores
    count = prune.shape[1]
    cap = 2 * part_rows * choose // (halves * peers)
    lo = lax.axis_index("lo").astype(jnp.int32)
    base = lax.axis_index("hi").astype(jnp.int32) * peers
    pieces = piece_count(peers)
    natural = jnp.stack([base, jnp.zeros_like(lo)])
    place = jnp.stack([base, lo if pieces == peers else jnp.zeros_like(lo)])
    across = [(i, (i + 1) % halves) for i in range(halves)]
    swap = [(i, (i + 1) % cores) for i in range(cores)]

    core_id = core.astype(jnp.int32).reshape(1)
    sent = cut(pixels, SENT_SHARE)
    first, last = sent[0][1], pixels - sent[0][1]
    given = cut(pixels, GIVEN_SHARE)
    payload = make_payload(core_id, particles, tau, candidates, prune, sent)
    far_payload = [lax.ppermute(chunk, "hi", across) for chunk in payload]

    sent_near, choice_near = pack(place, payload, pieces, peers, cap, choose)
    records_near = trade(sent_near, peers)

    other = lax.ppermute(projections, "ori", swap)
    own_views, other_views, norms = make_views(core_id, projections, other)
    far_payload[0], own_views = lax.optimization_barrier((far_payload[0], own_views))
    views = (own_views, other_views)

    sent_far, choice_far = pack(place, far_payload[:1], pieces, peers, cap, choose)
    records_near, sent_far = hold_back(records_near, sent_far, slice(1, 2))
    records_far = trade(sent_far, peers)
    choice_far, records_far[1 % len(records_far)] = lax.optimization_barrier(
        (choice_far, records_far[1 % len(records_far)])
    )
    rest_far = pack(place, far_payload[1:], pieces, peers, cap, choose, choice_far)
    rest_far, records_near = lax.optimization_barrier((rest_far, records_near))
    records_rest = trade(rest_far, peers)

    spans = ((last, 0, first), (0, first, last))
    near_mine = half_scores(records_near, *views, norms, spans, True)
    near_mine, records_rest = lax.optimization_barrier((near_mine, records_rest))

    mine = half_scores(records_far, *views, norms, ((0, 0, first),), True)
    mine = half_scores(records_rest, *views, norms, ((0, first, last),), False, mine)
    theirs = lax.ppermute(mine, "ori", swap)
    far_means, weights, inverse = weighted_means(mine, theirs, records_far, *views, given[0])
    near_theirs = lax.ppermute(near_mine, "ori", swap)
    near_theirs, far_means = lax.optimization_barrier((near_theirs, far_means))
    back_far = trade(far_means, peers)
    rest_means = rest_of_means(weights, inverse, *views, given[1], len(far_means))
    back_rest = trade(rest_means, peers)
    near_means, _, _ = weighted_means(near_mine, near_theirs, records_near, *views, (0, pixels))
    near_means, back_far = lax.optimization_barrier((near_means, back_far))
    far_mix, mixer = half_mix(choice_far, back_far)
    part_mix = lax.ppermute(far_mix, "hi", across)
    rest_mix = rest_of_mix(mixer, back_rest)
    rest_part = lax.ppermute(rest_mix, "hi", across)
    back_near = trade(near_means, peers)
    return final_mix(choice_near, back_near, (part_mix, rest_part), given)


def solution(mesh):
    grp, cls, ori = (mesh.shape[name] for name in ("grp", "cls", "ori"))
    inner = Mesh(mesh.devices.reshape(grp, 2, cls // 2, ori), ("grp", "hi", "lo", "ori"))
    rows = ("grp", "hi", "lo")
    placed = (
        P(rows, None),
        P(rows),
        P(rows, None),
        P(rows, "ori"),
        P(("hi", "lo"), "ori", None),
    )
    return jax.shard_map(
        on_device, mesh=inner, in_specs=placed, out_specs=P(rows, "ori"), check_vma=False
    )
```

```python
import functools

import jax
import jax.numpy as jnp
from jax import lax
from jax.experimental import pallas as pl
from jax.experimental.pallas import tpu as pltpu
from jax.sharding import Mesh
from jax.sharding import PartitionSpec as P

BOX = 128
LANES = 128
NEG = -1e30
shift_count = 5
GIVEN_SHARE = 4
SENT_SHARE = 5
VMEM_LIMIT = 24 * 1024 * 1024
IN_HBM = pl.BlockSpec(memory_space=pltpu.HBM)
IN_VMEM = pl.BlockSpec(memory_space=pltpu.VMEM)


def in_hbm(array):
    return pltpu.with_memory_space_constraint(array, pltpu.HBM)


def joined(refs, start, stop):
    if len(refs) == 1:
        return refs[0][:, start:stop]
    return jnp.concatenate([ref[:, start:stop] for ref in refs], axis=0)


def tiles_of(spans):
    tile = 32 * LANES
    for place, start, length in spans:
        for offset in range(0, length, tile):
            yield place + offset, start + offset, min(tile, length - offset)


def cut(pixels, *shares):
    ends = [pixels // 8 * share for share in shares] + [pixels]
    return tuple(zip([0] + ends[:-1], ends))


def piece_count(peers):
    return peers if peers <= 4 else 1


def split3(value):
    high = value.astype(jnp.bfloat16)
    rest = value - high.astype(jnp.float32)
    middle = rest.astype(jnp.bfloat16)
    low = (rest - middle.astype(jnp.float32)).astype(jnp.bfloat16)
    return high, middle, low


def put_log(value, rows):
    high, middle, low = split3(value)
    lane = lax.broadcasted_iota(jnp.int32, (rows, LANES), 1)
    pieces = jnp.where(
        lane == 0,
        high.astype(jnp.float32),
        jnp.where(
            lane == 1,
            middle.astype(jnp.float32),
            jnp.where(lane == 2, low.astype(jnp.float32), 0.0),
        ),
    )
    return pieces.astype(jnp.bfloat16)


def get_log(pieces):
    wide = pieces.astype(jnp.float32)
    return (wide[:, 0:1] + wide[:, 1:2]) + wide[:, 2:3]


def column_to_row(column, count):
    eye = lax.broadcasted_iota(jnp.int32, (count, count), 0) == lax.broadcasted_iota(
        jnp.int32, (count, count), 1
    )
    return jnp.sum(jnp.where(eye, column, 0.0), axis=0, keepdims=True)


def roll_lanes(block, amount):
    pieces = [
        pltpu.roll(block[:, start : start + LANES], amount % LANES, 1)
        for start in range(0, block.shape[1], LANES)
    ]
    return jnp.concatenate(pieces, axis=1)


def payload_kernel(
    core_ref, x_ref, tau_ref, classes_ref, keep_ref, *refs, chunks
):
    out_refs = refs[: len(chunks)]
    tau_scr, classes_scr, keep_scr, sems = refs[len(chunks) :]
    first_ref = out_refs[0]
    rows = first_ref.shape[0]
    count = keep_scr.shape[1]
    pixels = chunks[-1][1]
    copies = [
        pltpu.make_async_copy(tau_ref, tau_scr, sems.at[0]),
        pltpu.make_async_copy(classes_ref, classes_scr, sems.at[1]),
        pltpu.make_async_copy(keep_ref, keep_scr, sems.at[2]),
    ]
    for out_ref, (start, stop) in zip(out_refs, chunks):
        source = pl.multiple_of(core_ref[0] * pixels + start, LANES)
        copies.append(
            pltpu.make_async_copy(
                x_ref.at[:, pl.ds(source, stop - start)],
                out_ref.at[:, pl.ds(0, stop - start)],
                sems.at[len(copies)],
            )
        )
    for copy in copies:
        copy.start()
    for copy in copies[:3]:
        copy.wait()
    end = chunks[0][1]
    keep = keep_scr[...].astype(jnp.float32).astype(jnp.bfloat16)
    first_ref[:, end : end + count] = keep
    eye = lax.broadcasted_iota(jnp.int32, (rows, rows), 0) == lax.broadcasted_iota(
        jnp.int32, (rows, rows), 1
    )
    tau = jnp.sum(
        jnp.where(eye, tau_scr[...].astype(jnp.float32), 0.0), axis=1, keepdims=True
    )
    lane = lax.broadcasted_iota(jnp.int32, (rows, LANES), 1)
    meta = jnp.where(lane == 0, tau, 0.0)
    for j in range(classes_scr.shape[0]):
        named = classes_scr[j : j + 1, :].astype(jnp.float32)
        named = jnp.sum(jnp.where(eye, named, 0.0), axis=1, keepdims=True)
        meta = jnp.where(lane == 1 + j, named, meta)
    first_ref[:, end + count :] = meta.astype(jnp.bfloat16)
    for copy in copies[3:]:
        copy.wait()


def make_payload(core, particles, tau, candidates, prune, chunks):
    rows, choose = candidates.shape
    count = prune.shape[1]
    widths = [stop - start for start, stop in chunks]
    widths[0] += count + LANES
    return pl.pallas_call(
        functools.partial(payload_kernel, chunks=chunks),
        in_specs=[pl.BlockSpec(memory_space=pltpu.SMEM)] + [IN_HBM] * 4,
        out_specs=[IN_VMEM] * len(chunks),
        out_shape=[jax.ShapeDtypeStruct((rows, width), jnp.bfloat16) for width in widths],
        scratch_shapes=[
            pltpu.VMEM((1, rows), jnp.bfloat16),
            pltpu.VMEM((choose, rows), jnp.int32),
            pltpu.VMEM((rows, count), jnp.int32),
            pltpu.SemaphoreType.DMA((3 + len(chunks),)),
        ],
        compiler_params=pltpu.CompilerParams(vmem_limit_bytes=VMEM_LIMIT),
        name="make_payload",
    )(core, *(in_hbm(x) for x in (particles, tau.reshape(1, rows), candidates.T, prune)))


def choose_slots(meta, base, flip, classes, cap, choose):
    rows = meta.shape[0]
    slots = classes * cap
    ids = base + (lax.broadcasted_iota(jnp.int32, (rows, classes), 1) ^ flip)
    ids = ids.astype(jnp.float32)
    named = jnp.zeros((rows, classes), jnp.float32)
    for j in range(choose):
        named = jnp.where(meta[:, 1 + j : 2 + j] == ids, 1.0, named)
    earlier = (
        lax.broadcasted_iota(jnp.int32, (rows, rows), 0)
        > lax.broadcasted_iota(jnp.int32, (rows, rows), 1)
    ).astype(jnp.float32)
    rank = jnp.dot(earlier, named, preferred_element_type=jnp.float32)
    slot = lax.broadcasted_iota(jnp.int32, (classes, slots), 1)
    first = lax.broadcasted_iota(jnp.int32, (classes, slots), 0) * cap
    spread = ((slot >= first) & (slot < first + cap)).astype(jnp.float32)
    rank_at = jnp.dot(rank, spread, preferred_element_type=jnp.float32)
    named_at = jnp.dot(named, spread, preferred_element_type=jnp.float32)
    place = (lax.broadcasted_iota(jnp.int32, (rows, slots), 1) % cap).astype(jnp.float32)
    return jnp.where((named_at > 0.5) & (rank_at == place), 1.0, 0.0)


def pack_kernel(place_ref, *refs, sources, classes, cap, choose, known):
    x_refs = refs[:sources]
    if known:
        choice_ref = refs[sources]
        piece_refs = refs[sources + 1 :]
        choice = choice_ref[...]
    else:
        *piece_refs, choice_ref = refs[sources:]
        width = x_refs[0].shape[1]
        meta = x_refs[0][:, width - LANES :].astype(jnp.float32)
        choice = choose_slots(meta, place_ref[0], place_ref[1], classes, cap, choose)
        choice_ref[...] = choice
    picks = choice.astype(jnp.bfloat16)
    length = classes * cap // len(piece_refs)
    place = 0
    tile = 16 * LANES
    for x_ref in reversed(x_refs):
        width = x_ref.shape[1]
        for start in range(0, width, tile):
            stop = min(start + tile, width)
            packed = lax.dot_general(
                picks,
                x_ref[:, start:stop],
                (((0,), (0,)), ((), ())),
                preferred_element_type=jnp.float32,
            ).astype(jnp.bfloat16)
            for index, piece_ref in enumerate(piece_refs):
                piece_ref[:, place + start : place + stop] = packed[
                    index * length : (index + 1) * length
                ]
        place += width


def pack(place, chunks, pieces, classes, cap, choose, choice=None):
    rows = chunks[0].shape[0]
    width = sum(chunk.shape[1] for chunk in chunks)
    slots = classes * cap
    known = choice is not None
    outs = [jax.ShapeDtypeStruct((slots // pieces, width), jnp.bfloat16)] * pieces
    if not known:
        outs.append(jax.ShapeDtypeStruct((rows, slots), jnp.float32))
    args = [*chunks, choice] if known else chunks
    packed = pl.pallas_call(
        functools.partial(
            pack_kernel,
            sources=len(chunks),
            classes=classes,
            cap=cap,
            choose=choose,
            known=known,
        ),
        in_specs=[pl.BlockSpec(memory_space=pltpu.SMEM)] + [IN_VMEM] * len(args),
        out_specs=[IN_VMEM] * len(outs),
        out_shape=outs,
        compiler_params=pltpu.CompilerParams(vmem_limit_bytes=VMEM_LIMIT),
        name="pack_rest" if known else "pack",
    )(place, *args)
    return packed if known else (packed[:-1], packed[-1])


def views_kernel(core_ref, mine_ref, theirs_ref, own_ref, other_ref, norm_ref, rest, sems):
    core = core_ref[0]
    _, count, total = mine_ref.shape
    half = total // 2
    images = total // BOX
    before = (core * (images // 2) + images - 1) % images * BOX
    after = (core + 1) * (images // 2) % images * BOX
    copies = []

    def fetch(source_ref, source, target, length):
        source = pl.multiple_of(source, BOX)
        copy = pltpu.make_async_copy(
            source_ref.at[0, :, pl.ds(source, length)], target, sems.at[len(copies)]
        )
        copy.start()
        copies.append(copy)

    for source_ref, out_ref in ((mine_ref, own_ref), (theirs_ref, other_ref)):
        fetch(source_ref, core * half, out_ref.at[:, pl.ds(BOX, half)], half)
        fetch(source_ref, before, out_ref.at[:, pl.ds(0, BOX)], BOX)
        fetch(source_ref, after, out_ref.at[:, pl.ds(BOX + half, BOX)], BOX)
        if source_ref is mine_ref:
            fetch(source_ref, (1 - core) * half, rest, half)
    for copy in copies[:4]:
        copy.wait()
    sums = jnp.zeros((count, LANES), jnp.float32)
    for start in range(0, half, LANES):
        for piece in (own_ref[:, BOX + start : BOX + start + LANES], rest[:, start : start + LANES]):
            piece = piece.astype(jnp.float32)
            sums = sums + piece * piece
    norm_ref[...] = column_to_row(jnp.sum(sums, axis=1, keepdims=True), count)
    for copy in copies[4:]:
        copy.wait()


def make_views(core, mine, theirs):
    _, count, total = mine.shape
    ext = jax.ShapeDtypeStruct((count, total // 2 + 2 * BOX), jnp.bfloat16)
    return pl.pallas_call(
        views_kernel,
        in_specs=[pl.BlockSpec(memory_space=pltpu.SMEM), IN_HBM, IN_HBM],
        out_specs=[IN_VMEM, IN_VMEM, IN_VMEM],
        out_shape=[ext, ext, jax.ShapeDtypeStruct((1, count), jnp.float32)],
        scratch_shapes=[
            pltpu.VMEM((count, total // 2), jnp.bfloat16),
            pltpu.SemaphoreType.DMA((7,)),
        ],
        compiler_params=pltpu.CompilerParams(vmem_limit_bytes=VMEM_LIMIT),
        name="make_views",
    )(core, in_hbm(mine), in_hbm(theirs))


def score_kernel(*refs, pieces, spans, masked, added):
    x_refs = refs[:pieces]
    own_ref, other_ref, norm_ref = refs[pieces : pieces + 3]
    out_ref = refs[-1]
    rows = sum(ref.shape[0] for ref in x_refs)
    count = own_ref.shape[0]
    span = 2 * count
    one = jnp.zeros((rows, LANES), jnp.bfloat16)
    two = jnp.zeros((rows, 2 * LANES), jnp.bfloat16)
    total = None
    for place, start, tile in tiles_of(spans):
        image = joined(x_refs, place, place + tile)
        stack = [
            [one, image, one],
            [image, two],
            [two, image],
            [one, roll_lanes(image, -1), one],
            [one, roll_lanes(image, 1), one],
        ]
        stack = jnp.concatenate([jnp.concatenate(line, axis=1) for line in stack], axis=0)
        stop = start + tile + 2 * LANES
        both = jnp.concatenate([own_ref[:, start:stop], other_ref[:, start:stop]], axis=0)
        part = lax.dot_general(
            stack, both, (((1,), (1,)), ((), ())), preferred_element_type=jnp.float32
        )
        total = part if total is None else total + part
    if masked:
        width = x_refs[0].shape[1]
        keep = joined(x_refs, width - LANES - count, width - LANES).astype(jnp.float32)
        offset = jnp.where(keep > 0.5, 0.0, NEG) - 0.5 * norm_ref[...]
        offset = jnp.concatenate([offset, jnp.zeros_like(offset)], axis=1)
    for index in range(shift_count):
        block = slice(index * span, (index + 1) * span)
        value = total[index * rows : (index + 1) * rows]
        if masked:
            value = value + offset
        if added:
            value = value + refs[pieces + 3][:, block]
        out_ref[:, block] = value


def half_scores(records, own, other, norms, spans, masked, earlier=None):
    rows = sum(piece.shape[0] for piece in records)
    count = own.shape[0]
    args = [*records, own, other, norms]
    if earlier is not None:
        args.append(earlier)
    return pl.pallas_call(
        functools.partial(
            score_kernel,
            pieces=len(records),
            spans=spans,
            masked=masked,
            added=earlier is not None,
        ),
        in_specs=[IN_VMEM] * len(args),
        out_specs=IN_VMEM,
        out_shape=jax.ShapeDtypeStruct((rows, 2 * shift_count * count), jnp.float32),
        compiler_params=pltpu.CompilerParams(vmem_limit_bytes=VMEM_LIMIT),
        name="half_scores",
    )(*args)


def weigh(mine_ref, theirs_ref, tau, count, weight_ref):
    rows = tau.shape[0]
    span = 2 * count
    scores = []
    peak = jnp.full((rows, 1), NEG, jnp.float32)
    for index in range(shift_count):
        mine = mine_ref[:, index * span : (index + 1) * span]
        theirs = theirs_ref[:, index * span : (index + 1) * span]
        swapped = jnp.concatenate([theirs[:, count:], theirs[:, :count]], axis=1)
        full = mine + swapped
        score = jnp.where(full > -1e29, tau * full, NEG)
        scores.append(score)
        peak = jnp.maximum(peak, jnp.max(score, axis=1, keepdims=True))
    total = jnp.zeros((rows, 1), jnp.float32)
    for index, score in enumerate(scores):
        weight = jnp.where(score > -1e28, jnp.exp(score - peak), 0.0).astype(jnp.bfloat16)
        total = total + jnp.sum(weight.astype(jnp.float32), axis=1, keepdims=True)
        weight_ref[index * rows : (index + 1) * rows, :] = weight
    filled = total > 0
    safe = jnp.where(filled, total, 1.0)
    return 1.0 / safe, put_log(jnp.where(filled, peak + jnp.log(safe), NEG), rows)


def write_means(weight_ref, inverse, own_ref, other_ref, out_refs, start, stop):
    length = out_refs[0].shape[0]
    rows = length * len(out_refs)
    weights = weight_ref[...]
    for place, first, tile in tiles_of([(0, start, stop - start)]):
        end = first + tile + 2 * LANES
        both = jnp.concatenate([own_ref[:, first:end], other_ref[:, first:end]], axis=0)
        sums = jnp.dot(weights, both, preferred_element_type=jnp.float32)
        inner = slice(LANES, LANES + tile)
        mean = sums[0:rows, inner] + sums[rows : 2 * rows, 0:tile]
        mean = mean + sums[2 * rows : 3 * rows, 2 * LANES : 2 * LANES + tile]
        mean = mean + roll_lanes(sums[3 * rows : 4 * rows, inner], 1)
        mean = mean + roll_lanes(sums[4 * rows : 5 * rows, inner], -1)
        mean = (mean * inverse).astype(jnp.bfloat16)
        for index, out_ref in enumerate(out_refs):
            out_ref[:, place : place + tile] = mean[index * length : (index + 1) * length]


def mean_kernel(mine_ref, theirs_ref, *refs, chunk, pieces):
    x_refs = refs[:pieces]
    own_ref, other_ref = refs[pieces : pieces + 2]
    out_refs = refs[pieces + 2 : 2 * pieces + 2]
    weight_ref, inverse_ref = refs[2 * pieces + 2 :]
    length, width = x_refs[0].shape
    tau = joined(x_refs, width - LANES, width)[:, 0:1].astype(jnp.float32)
    inverse, logs = weigh(mine_ref, theirs_ref, tau, own_ref.shape[0], weight_ref)
    inverse_ref[...] = jnp.broadcast_to(inverse, inverse_ref.shape)
    start, stop = chunk
    for index, out_ref in enumerate(out_refs):
        out_ref[:, stop - start :] = logs[index * length : (index + 1) * length]
    write_means(weight_ref, inverse, own_ref, other_ref, out_refs, start, stop)


def weighted_means(mine, theirs, records, own, other, chunk):
    length = records[0].shape[0]
    pieces = len(records)
    count = own.shape[0]
    outs = [jax.ShapeDtypeStruct((length, chunk[1] - chunk[0] + LANES), jnp.bfloat16)] * pieces
    outs += [
        jax.ShapeDtypeStruct((shift_count * pieces * length, 2 * count), jnp.bfloat16),
        jax.ShapeDtypeStruct((pieces * length, LANES), jnp.float32),
    ]
    *means, weights, inverse = pl.pallas_call(
        functools.partial(mean_kernel, chunk=chunk, pieces=pieces),
        in_specs=[IN_VMEM] * (pieces + 4),
        out_specs=[IN_VMEM] * len(outs),
        out_shape=outs,
        compiler_params=pltpu.CompilerParams(vmem_limit_bytes=VMEM_LIMIT),
        name="weighted_means",
    )(mine, theirs, *records, own, other)
    return means, weights, inverse


def rest_kernel(weight_ref, inverse_ref, own_ref, other_ref, *out_refs, chunk):
    write_means(weight_ref, inverse_ref[:, 0:1], own_ref, other_ref, out_refs, *chunk)


def rest_of_means(weights, inverse, own, other, chunk, pieces):
    length = inverse.shape[0] // pieces
    return pl.pallas_call(
        functools.partial(rest_kernel, chunk=chunk),
        in_specs=[IN_VMEM] * 4,
        out_specs=[IN_VMEM] * pieces,
        out_shape=[jax.ShapeDtypeStruct((length, chunk[1] - chunk[0]), jnp.bfloat16)] * pieces,
        compiler_params=pltpu.CompilerParams(vmem_limit_bytes=VMEM_LIMIT),
        name="rest_of_means",
    )(weights, inverse, own, other)


def half_mix_kernel(choice_ref, *refs, pieces):
    back_refs = refs[:pieces]
    out_ref, mixer_ref = refs[pieces:]
    rows, slots = choice_ref.shape
    width = out_ref.shape[1] - LANES
    chosen = choice_ref[...] > 0.5
    row = column_to_row(get_log(joined(back_refs, width, width + LANES)), slots)
    value = jnp.where(chosen, row, NEG)
    best = jnp.max(value, axis=1, keepdims=True)
    factor = jnp.where(chosen, jnp.exp(value - best), 0.0)
    total = jnp.sum(factor, axis=1, keepdims=True)
    filled = total > 0
    safe = jnp.where(filled, total, 1.0)
    mixer = jnp.concatenate(split3(factor / safe), axis=0)
    mixer_ref[...] = mixer
    out_ref[:, width:] = put_log(jnp.where(filled, best + jnp.log(safe), NEG), rows)
    write_mix(mixer, back_refs, out_ref, width)


def write_mix(mixer, back_refs, out_ref, width):
    rows = out_ref.shape[0]
    for place, _, tile in tiles_of([(0, 0, width)]):
        images = joined(back_refs, place, place + tile)
        mixed = jnp.dot(mixer, images, preferred_element_type=jnp.float32)
        mixed = mixed[0:rows] + (mixed[rows : 2 * rows] + mixed[2 * rows : 3 * rows])
        out_ref[:, place : place + tile] = mixed.astype(jnp.bfloat16)


def rest_mix_kernel(mixer_ref, *refs):
    *back_refs, out_ref = refs
    write_mix(mixer_ref[...], back_refs, out_ref, out_ref.shape[1])


def half_mix(choice, back):
    rows, slots = choice.shape
    return pl.pallas_call(
        functools.partial(half_mix_kernel, pieces=len(back)),
        in_specs=[IN_VMEM] * (1 + len(back)),
        out_specs=[IN_VMEM] * 2,
        out_shape=[
            jax.ShapeDtypeStruct((rows, back[0].shape[1]), jnp.bfloat16),
            jax.ShapeDtypeStruct((3 * rows, slots), jnp.bfloat16),
        ],
        compiler_params=pltpu.CompilerParams(vmem_limit_bytes=VMEM_LIMIT),
        name="half_mix",
    )(choice, *back)


def rest_of_mix(mixer, back):
    rows = mixer.shape[0] // 3
    return pl.pallas_call(
        rest_mix_kernel,
        in_specs=[IN_VMEM] * (1 + len(back)),
        out_specs=IN_VMEM,
        out_shape=jax.ShapeDtypeStruct((rows, back[0].shape[1]), jnp.bfloat16),
        compiler_params=pltpu.CompilerParams(vmem_limit_bytes=VMEM_LIMIT),
        name="rest_of_mix",
    )(mixer, *back)


def final_kernel(choice_ref, *refs, pieces, chunks):
    back_refs = refs[:pieces]
    *part_refs, out_ref, mixed_ref, sems = refs[pieces:]
    copies = []
    rows, slots = choice_ref.shape
    pixels = chunks[-1][1]
    end = chunks[0][1]
    chosen = choice_ref[...] > 0.5
    row = column_to_row(get_log(joined(back_refs, pixels, pixels + LANES)), slots)
    value = jnp.where(chosen, row, NEG)
    part = get_log(part_refs[0][:, end:])
    best = jnp.maximum(jnp.max(value, axis=1, keepdims=True), part)
    factor = jnp.where(chosen, jnp.exp(value - best), 0.0)
    part_factor = jnp.where(part > -1e29, jnp.exp(part - best), 0.0)
    total = jnp.sum(factor, axis=1, keepdims=True) + part_factor
    safe = jnp.where(total > 0, total, 1.0)
    part_factor = part_factor / safe
    mixer = jnp.concatenate(split3(factor / safe), axis=0)
    for (first, last), part_ref in zip(chunks, part_refs):
        for place, start, tile in tiles_of([(0, first, last - first)]):
            images = joined(back_refs, start, start + tile)
            mixed = jnp.dot(mixer, images, preferred_element_type=jnp.float32)
            mixed = mixed[0:rows] + (mixed[rows : 2 * rows] + mixed[2 * rows : 3 * rows])
            mixed = mixed + part_factor * part_ref[:, place : place + tile].astype(jnp.float32)
            span = pl.ds(start, tile)
            mixed_ref[:, span] = mixed.astype(jnp.bfloat16)
            copy = pltpu.make_async_copy(
                mixed_ref.at[:, span], out_ref.at[:, span], sems.at[len(copies)]
            )
            copy.start()
            copies.append(copy)
    for copy in copies:
        copy.wait()


def final_mix(choice, back, parts, chunks):
    rows = choice.shape[0]
    args = [choice, *back, *parts]
    count = len(list(tiles_of([(0, first, last - first) for first, last in chunks])))
    return pl.pallas_call(
        functools.partial(final_kernel, pieces=len(back), chunks=chunks),
        in_specs=[IN_VMEM] * len(args),
        out_specs=IN_HBM,
        out_shape=jax.ShapeDtypeStruct((rows, chunks[-1][1]), jnp.bfloat16),
        scratch_shapes=[
            pltpu.VMEM((rows, chunks[-1][1]), jnp.bfloat16),
            pltpu.SemaphoreType.DMA((count,)),
        ],
        compiler_params=pltpu.CompilerParams(vmem_limit_bytes=VMEM_LIMIT),
        name="final_mix",
    )(*args)


def trade(pieces, peers):
    if len(pieces) == peers:
        return [pieces[0]] + [
            lax.ppermute(pieces[flip], "lo", [(i, i ^ flip) for i in range(peers)])
            for flip in range(1, peers)
        ]
    whole = pieces[0]
    parts = whole.reshape(peers, whole.shape[0] // peers, whole.shape[1])
    parts = lax.all_to_all(parts, "lo", split_axis=0, concat_axis=0, tiled=True)
    return [parts.reshape(whole.shape)]


def hold_back(early, late, part):
    held, late = lax.optimization_barrier((early[part], late))
    early = list(early)
    early[part] = held
    return early, late


def on_device(particles, tau, candidates, prune, projections):
    halves = lax.axis_size("hi")
    peers = lax.axis_size("lo")
    cores = lax.axis_size("ori")
    core = lax.axis_index("ori")
    part_rows, choose = candidates.shape
    pixels = particles.shape[1] // cores
    count = prune.shape[1]
    cap = 2 * part_rows * choose // (halves * peers)
    lo = lax.axis_index("lo").astype(jnp.int32)
    base = lax.axis_index("hi").astype(jnp.int32) * peers
    pieces = piece_count(peers)
    natural = jnp.stack([base, jnp.zeros_like(lo)])
    place = jnp.stack([base, lo if pieces == peers else jnp.zeros_like(lo)])
    across = [(i, (i + 1) % halves) for i in range(halves)]
    swap = [(i, (i + 1) % cores) for i in range(cores)]

    core_id = core.astype(jnp.int32).reshape(1)
    sent = cut(pixels, SENT_SHARE)
    first, last = sent[0][1], pixels - sent[0][1]
    given = cut(pixels, GIVEN_SHARE)
    payload = make_payload(core_id, particles, tau, candidates, prune, sent)
    far_payload = [lax.ppermute(chunk, "hi", across) for chunk in payload]

    sent_near, choice_near = pack(place, payload, pieces, peers, cap, choose)
    records_near = trade(sent_near, peers)

    other = lax.ppermute(projections, "ori", swap)
    own_views, other_views, norms = make_views(core_id, projections, other)
    far_payload[0], own_views = lax.optimization_barrier((far_payload[0], own_views))
    views = (own_views, other_views)

    sent_far, choice_far = pack(place, far_payload[:1], pieces, peers, cap, choose)
    records_near, sent_far = hold_back(records_near, sent_far, slice(1, 2))
    records_far = trade(sent_far, peers)
    choice_far, records_far[1 % len(records_far)] = lax.optimization_barrier(
        (choice_far, records_far[1 % len(records_far)])
    )
    rest_far = pack(place, far_payload[1:], pieces, peers, cap, choose, choice_far)
    rest_far, records_near = lax.optimization_barrier((rest_far, records_near))
    records_rest = trade(rest_far, peers)

    spans = ((last, 0, first), (0, first, last))
    near_mine = half_scores(records_near, *views, norms, spans, True)
    near_mine, records_rest = lax.optimization_barrier((near_mine, records_rest))

    mine = half_scores(records_far, *views, norms, ((0, 0, first),), True)
    mine = half_scores(records_rest, *views, norms, ((0, first, last),), False, mine)
    theirs = lax.ppermute(mine, "ori", swap)
    far_means, weights, inverse = weighted_means(mine, theirs, records_far, *views, given[0])
    near_theirs = lax.ppermute(near_mine, "ori", swap)
    back_far = trade(far_means, peers)
    rest_means = rest_of_means(weights, inverse, *views, given[1], len(far_means))
    back_rest = trade(rest_means, peers)
    near_means, _, _ = weighted_means(near_mine, near_theirs, records_near, *views, (0, pixels))
    near_means, back_far = lax.optimization_barrier((near_means, back_far))
    far_mix, mixer = half_mix(choice_far, back_far)
    part_mix = lax.ppermute(far_mix, "hi", across)
    rest_mix = rest_of_mix(mixer, back_rest)
    rest_part = lax.ppermute(rest_mix, "hi", across)
    back_near = trade(near_means, peers)
    return final_mix(choice_near, back_near, (part_mix, rest_part), given)


def solution(mesh):
    grp, cls, ori = (mesh.shape[name] for name in ("grp", "cls", "ori"))
    inner = Mesh(mesh.devices.reshape(grp, 2, cls // 2, ori), ("grp", "hi", "lo", "ori"))
    rows = ("grp", "hi", "lo")
    placed = (
        P(rows, None),
        P(rows),
        P(rows, None),
        P(rows, "ori"),
        P(("hi", "lo"), "ori", None),
    )
    return jax.shard_map(
        on_device, mesh=inner, in_specs=placed, out_specs=P(rows, "ori"), check_vma=False
    )
```
